128 devices in a mesh: cfg: 2 (over core), lat: 4 (over x), seq: 16 (over z, y).
Axes of the slice: x: 4, y: 4, z: 4, core: 2. Of those that a mesh axis runs over, the one named last changes fastest.
Arguments:
- latents: float32 [24, 1024, 16], P('lat', 'seq'), may hold values from -6 to 6
- timesteps: int32 [24], P('lat'), may hold values from 0 to 999
- labels: int32 [24], P('lat'), may hold values from 0 to 999
- guidance: float32 [1], replicated, may hold values from 1.5 to 4
- keep_coef: float32 [24], P('lat'), may hold values from 0.8 to 1.2
- noise_coef: float32 [24], P('lat'), may hold values from -0.6 to -0.2
- w_patch: bfloat16 [16, 1152], replicated, may hold values from -1.5 to 1.5
- label_table: bfloat16 [1001, 1152], replicated, may hold values from -6 to 6
- w_time1: bfloat16 [256, 1152], P(None, 'lat'), may hold values from -0.375 to 0.375
- w_time2: bfloat16 [1152, 1152], P(None, 'lat'), may hold values from -0.1875 to 0.1875
- ada_weight: bfloat16 [1152, 9216], P(None, 'seq'), may hold values from -0.1875 to 0.1875
- w_qkv: bfloat16 [1152, 3456], P(None, 'seq'), may hold values from -2.9168155 to 2.9168155
- w_proj: bfloat16 [1152, 1152], P(None, 'seq'), may hold values from -0.1875 to 0.1875
- w_fc1: bfloat16 [1152, 4608], P(None, 'seq'), may hold values from -0.1875 to 0.1875
- w_fc2: bfloat16 [4608, 1152], P('seq'), may hold values from -0.09375 to 0.09375
- w_out: bfloat16 [1152, 16], replicated, may hold values from -0.1875 to 0.1875
Outputs:
- next_latents: float32 [24, 1024, 16], P('lat', 'seq', 'cfg')
The draws below stay inside these ranges and needn't reach their ends.
All inputs are finite; a program needn't handle non-finite values.
Results may differ from the reference program's by a relative error of at most 0.009.
Values may be sent and summed in bfloat16 or wider, within the bound.
A program may use at most 192 MiB of HBM per device.

```python
import math
import jax
import jax.numpy as jnp
from jax import lax

D = 1152
HEADS = 16
HEAD_DIM = 72
FF = 4608
CLASSES = 1000
FREQ = 256
PATCH_CH = 16
GRID = 32
STEPS = 1000
TOKENS = 1024
LATENTS = 24


def draw_w_qkv(key, part):
    normals = jnp.clip(jax.random.normal(key, (D, 3 * D), jnp.float32), -6.0, 6.0)
    query_part = normals[:, :D]
    key_part = normals[:, D:2 * D]
    value_part = normals[:, 2 * D:]
    whole = jnp.concatenate([query_part, key_part, value_part], axis=1) * D ** (-0.5)
    return whole.astype(jnp.bfloat16)


def place_ends(drawn, rng, low, top_value):
    dims = drawn.shape
    spot = [jax.random.randint(jax.random.fold_in(rng, axis), (), 0, dims[axis]) for axis in range(len(dims))]
    drawn = drawn.at[tuple(spot)].set(low)
    longest = dims.index(max(dims))
    spot[longest] = (spot[longest] + 1) % dims[longest]
    return drawn.at[tuple(spot)].set(top_value)


def level_of(rng, extent, cuts, least, high):
    def one(position, parts):
        steps = jax.random.uniform(jax.random.fold_in(jax.random.fold_in(rng, 6), position), (parts,), jnp.float32, least / len(cuts), high / len(cuts))
        return jnp.repeat(jnp.exp(steps), extent[position] // parts).reshape((-1,) + (1,) * (len(extent) - position - 1))

    loudness = one(*cuts[0])
    for cut in cuts[1:]:
        loudness = loudness * one(*cut)
    return loudness


def gaussian(rng, dims, width, most, split=(), held_as=jnp.bfloat16):
    result = width * jax.random.normal(rng, dims, jnp.float32)
    if split:
        result = result * level_of(rng, dims, split, -0.22, 0.18)
    return jnp.clip(result, -most, most).astype(held_as)


def setup_inputs(seed: int = 0) -> dict:
    streams_of = jax.random.split(jax.random.key(seed), 17)
    latents = gaussian(streams_of[0], (LATENTS, TOKENS, PATCH_CH), 1.0, 6.0, ((0, 4), (1, 16)), jnp.float32)
    timesteps = place_ends(jax.random.randint(streams_of[1], (LATENTS,), 0, STEPS), jax.random.fold_in(streams_of[1], 1), 0, STEPS - 1).astype(jnp.int32)
    labels = place_ends(jax.random.randint(streams_of[2], (LATENTS,), 0, CLASSES), jax.random.fold_in(streams_of[2], 1), 0, CLASSES - 1).astype(jnp.int32)
    guidance = jnp.clip(jax.random.uniform(streams_of[3], (1,), jnp.float32, 1.5, 4.0), 1.5, 4.0)
    keep_coef = jnp.clip(0.8 + 0.40000004 * jax.random.uniform(streams_of[4], (LATENTS,), jnp.float32) ** level_of(streams_of[4], (LATENTS,), ((0, 4),), -0.2, 0.2), 0.8, 1.2)
    noise_coef = jnp.clip(-0.6 + 0.400000021 * jax.random.uniform(streams_of[5], (LATENTS,), jnp.float32) ** level_of(streams_of[5], (LATENTS,), ((0, 4),), -0.2, 0.2), -0.6, -0.2)
    w_patch = gaussian(streams_of[6], (PATCH_CH, D), PATCH_CH ** -0.5, 1.5)
    label_table = gaussian(streams_of[7], (CLASSES + 1, D), 1.0, 6.0)
    w_time1 = gaussian(streams_of[8], (FREQ, D), FREQ ** -0.5, 0.375, ((1, 4),))
    w_time2 = gaussian(streams_of[9], (D, D), D ** -0.5, 0.1875, ((1, 4),))
    ada_weight = gaussian(streams_of[10], (D, 8 * D), D ** -0.5, 0.1875, ((1, 16),))
    w_qkv = draw_w_qkv(jax.random.fold_in(streams_of[16], 71), 0)
    w_proj = gaussian(streams_of[12], (D, D), D ** -0.5, 0.1875, ((1, 16),))
    w_fc1 = gaussian(streams_of[13], (D, FF), D ** -0.5, 0.1875, ((1, 16),))
    w_fc2 = gaussian(streams_of[14], (FF, D), FF ** -0.5, 0.09375, ((0, 16),))
    w_out = gaussian(streams_of[15], (D, PATCH_CH), D ** -0.5, 0.1875)
    return {"latents": latents, "timesteps": timesteps, "labels": labels, "guidance": guidance, "keep_coef": keep_coef, "noise_coef": noise_coef, "w_patch": w_patch, "label_table": label_table, "w_time1": w_time1, "w_time2": w_time2, "ada_weight": ada_weight, "w_qkv": w_qkv, "w_proj": w_proj, "w_fc1": w_fc1, "w_fc2": w_fc2, "w_out": w_out}


def layer_norm(values):
    average = lax.optimization_barrier(jnp.mean(values, axis=-1, keepdims=True))
    centered = values - average
    spread = lax.optimization_barrier(jnp.mean(centered * centered, axis=-1, keepdims=True))
    return centered * lax.rsqrt(spread + 1e-06)

def modulate(values, shifted, scaled):
    return layer_norm(values) * (1.0 + scaled[:, None, :]) + shifted[:, None, :]

def time_waves(timesteps):
    half_count = FREQ // 2
    frequency = jnp.exp(-math.log(10000.0) * jnp.arange(half_count, dtype=jnp.float32) / half_count)
    angles = timesteps.astype(jnp.float32)[:, None] * frequency[None, :]
    return jnp.concatenate([jnp.cos(angles), jnp.sin(angles)], axis=-1)

def grid_waves(positions):
    quarter = D // 4
    frequency = jnp.exp(-math.log(10000.0) * jnp.arange(quarter, dtype=jnp.float32) / quarter)
    column = (positions % GRID).astype(jnp.float32)[:, None] * frequency[None, :]
    row_angle = (positions // GRID).astype(jnp.float32)[:, None] * frequency[None, :]
    return jnp.concatenate([jnp.sin(column), jnp.cos(column), jnp.sin(row_angle), jnp.cos(row_angle)], axis=-1)

def condition(timesteps, classes, label_table, w_time1, w_time2):
    waves = time_waves(timesteps).astype(jnp.bfloat16)
    hidden_time = jax.nn.silu(jnp.dot(waves, w_time1, preferred_element_type=jnp.float32)).astype(jnp.bfloat16)
    time_vector = jnp.dot(hidden_time, w_time2, preferred_element_type=jnp.float32)
    onehot = (classes[:, None] == jnp.arange(CLASSES + 1, dtype=jnp.int32)[None, :]).astype(jnp.bfloat16)
    return time_vector + jnp.dot(onehot, label_table, preferred_element_type=jnp.float32)

def attend_latent(operands):
    queries, keys_all, values_all = operands
    factor = 1.0 / math.sqrt(HEAD_DIM)
    scores = jnp.einsum('qhd,khd->hqk', queries.astype(jnp.float32), keys_all.astype(jnp.float32)) * factor
    row_peak = lax.optimization_barrier(jnp.max(scores, axis=-1, keepdims=True))
    exponent = jnp.exp(scores - row_peak)
    denominator = lax.optimization_barrier(jnp.sum(exponent, axis=-1))
    attn_weights = exponent.astype(jnp.bfloat16)
    mixed = jnp.einsum('hqk,khd->hqd', attn_weights.astype(jnp.float32), values_all.astype(jnp.float32)) / denominator[..., None]
    return jnp.transpose(mixed, (1, 0, 2)).reshape(TOKENS, D).astype(jnp.bfloat16)

def forward(latents, conditioning, w_patch, ada_weight, w_qkv, w_proj, w_fc1, w_fc2, w_out):
    latent_count = latents.shape[0]
    modulation = jnp.dot(jax.nn.silu(conditioning).astype(jnp.bfloat16), ada_weight, preferred_element_type=jnp.float32)
    pieces = [modulation[:, number * D:(number + 1) * D] for number in range(8)]
    positions = jnp.arange(TOKENS, dtype=jnp.int32)
    state = jnp.dot(latents.reshape(-1, PATCH_CH).astype(jnp.bfloat16), w_patch, preferred_element_type=jnp.float32)
    state = state.reshape(latent_count, TOKENS, D) + grid_waves(positions)[None]
    normed = modulate(state, pieces[0], pieces[1]).astype(jnp.bfloat16).reshape(-1, D)
    triple = jnp.dot(normed, w_qkv, preferred_element_type=jnp.float32).astype(jnp.bfloat16)
    triple = triple.reshape(latent_count, TOKENS, 3, HEADS, HEAD_DIM)
    attended = lax.map(attend_latent, (triple[:, :, 0], triple[:, :, 1], triple[:, :, 2]))
    projected = jnp.dot(attended.reshape(-1, D), w_proj, preferred_element_type=jnp.float32)
    state = state + pieces[2][:, None, :] * projected.reshape(latent_count, TOKENS, D)
    normed = modulate(state, pieces[3], pieces[4]).astype(jnp.bfloat16).reshape(-1, D)
    hidden = jax.nn.gelu(jnp.dot(normed, w_fc1, preferred_element_type=jnp.float32), approximate=True).astype(jnp.bfloat16)
    mlp_out = jnp.dot(hidden, w_fc2, preferred_element_type=jnp.float32)
    state = state + pieces[5][:, None, :] * mlp_out.reshape(latent_count, TOKENS, D)
    final = modulate(state, pieces[6], pieces[7]).astype(jnp.bfloat16).reshape(-1, D)
    return jnp.dot(final, w_out, preferred_element_type=jnp.float32).reshape(latent_count, TOKENS, PATCH_CH)

def reference(latents, timesteps, labels, guidance, keep_coef, noise_coef, w_patch, label_table, w_time1, w_time2, ada_weight, w_qkv, w_proj, w_fc1, w_fc2, w_out):
    cond_vector = condition(timesteps, labels, label_table, w_time1, w_time2)
    null_labels = jnp.full_like(labels, CLASSES)
    free_vector = condition(timesteps, null_labels, label_table, w_time1, w_time2)
    cond_noise = forward(latents, cond_vector, w_patch, ada_weight, w_qkv, w_proj, w_fc1, w_fc2, w_out)
    free_noise = forward(latents, free_vector, w_patch, ada_weight, w_qkv, w_proj, w_fc1, w_fc2, w_out)
    guided = free_noise + guidance[0] * (cond_noise - free_noise)
    return keep_coef[:, None, None] * latents + noise_coef[:, None, None] * guided
```

```python
import math

import jax
import jax.numpy as jnp
import numpy as np
from jax import lax
from jax.experimental import pallas as pl
from jax.experimental.pallas import tpu as pltpu
from jax.sharding import PartitionSpec as P

D = 1152
HEADS = 16
HEAD_DIM = 72
CLASSES = 1000
FREQ = 256
GRID = 32
TOKENS = 1024
BASE = 16 + 2 * GRID
ROWS = 96
LANES = 128
Q_ROWS = 256
F32 = jnp.float32
BF16 = jnp.bfloat16
NT = (((1,), (1,)), ((), ()))
NN = (((1,), (0,)), ((), ()))
HIGH = lax.Precision.HIGHEST


def position_rows():
    quarter = D // 4
    frequency = np.exp(-math.log(10000.0) * np.arange(quarter) / quarter)
    angle = np.arange(GRID)[:, None] * frequency[None, :]
    waves = np.concatenate([np.sin(angle), np.cos(angle)], axis=1)
    rows = np.zeros((2 * GRID, D))
    rows[:GRID, : D // 2] = waves
    rows[GRID:, D // 2 :] = waves
    return rows


def dot(a, b, dims=NN, precision=None):
    return lax.dot_general(a, b, dims, precision=precision, preferred_element_type=F32)


def layer_norm(values):
    average = jnp.mean(values, axis=-1, keepdims=True)
    centered = values - average
    spread = jnp.mean(centered * centered, axis=-1, keepdims=True)
    return centered * lax.rsqrt(spread + 1e-06)


def time_waves(timesteps):
    half_count = FREQ // 2
    frequency = jnp.exp(-math.log(10000.0) * jnp.arange(half_count, dtype=F32) / half_count)
    angles = timesteps.astype(F32)[:, None] * frequency[None, :]
    return jnp.concatenate([jnp.cos(angles), jnp.sin(angles)], axis=-1)


def attend_kernel(
    lat_ref, patch_ref, pos_ref, shift_ref, scale_ref, wq_ref, wk_ref, wv_ref,
    out_ref, ft_ref, base_ref, xs_ref, tq_ref, tv_ref, tk_ref, rstd_ref, rcol_ref, q_ref, v_ref, kt_ref,
):
    count = lat_ref.shape[0]
    patch = patch_ref[...].astype(F32)
    base_ref[:16, :] = patch - jnp.mean(patch, axis=1, keepdims=True)
    base_ref[16:, :] = pos_ref[...]
    base = base_ref[...]
    gram = dot(base, base, NT, HIGH) * (1.0 / D)
    token = lax.broadcasted_iota(jnp.int32, (2 * GRID, TOKENS), 1)
    place = lax.broadcasted_iota(jnp.int32, (2 * GRID, TOKENS), 0)
    hot = jnp.where(jnp.where(place < GRID, token % GRID, token // GRID + GRID) == place, 1.0, 0.0).astype(BF16)
    rstd_ref[...] = jnp.zeros_like(rstd_ref)
    for l in range(count):
        ft_ref[l, :16, :] = lat_ref[l]
        ft_ref[l, 16:, :] = hot
        ft = ft_ref[l].astype(F32)
        spread = jnp.sum(dot(gram, ft, NN, HIGH) * ft, axis=0, keepdims=True)
        rstd_ref[l : l + 1, :] = lax.rsqrt(spread + 1e-06)
        xs_ref[l * ROWS : l * ROWS + BASE, :] = (base * (1.0 + scale_ref[l : l + 1, :])).astype(BF16)
        xs_ref[l * ROWS + BASE : (l + 1) * ROWS, :] = jnp.broadcast_to(
            shift_ref[l : l + 1, :], (ROWS - BASE, D)
        ).astype(BF16)
    rcol_ref[...] = jnp.transpose(rstd_ref[...])
    factor = math.log2(math.e) / math.sqrt(HEAD_DIM)
    tq_ref[...] = dot(xs_ref[...], wq_ref[...], NT) * factor
    tv_ref[...] = dot(xs_ref[...], wv_ref[...], NT)
    for l in range(count):
        tk_ref[l] = dot(wk_ref[...], xs_ref[l * ROWS : (l + 1) * ROWS, :], NT)
    ones_lane = lax.broadcasted_iota(jnp.int32, (TOKENS, LANES), 1) == HEAD_DIM
    v_ref[...] = jnp.where(ones_lane, 1.0, 0.0).astype(BF16)

    def one_latent(l, carry):
        ft = ft_ref[l]
        f = jnp.transpose(ft.astype(F32)).astype(BF16)
        lane = lax.broadcasted_iota(jnp.int32, (TOKENS, LANES), 1)
        column = jnp.sum(jnp.where(lane == l, rcol_ref[...], 0.0), axis=1, keepdims=True)
        top = pl.multiple_of(l * ROWS, ROWS)
        tq = tq_ref[pl.ds(top, ROWS), :]
        tv = tv_ref[pl.ds(top, ROWS), :]
        tk = tk_ref[l]
        q_ref[...] = (dot(f, tq[:BASE].astype(BF16)) * column + tq[BASE : BASE + 1]).astype(BF16)
        v_ref[:, :HEAD_DIM] = (dot(f, tv[:BASE].astype(BF16)) * column + tv[BASE : BASE + 1]).astype(BF16)
        kt_ref[...] = (
            dot(tk[:, :BASE].astype(BF16), ft) * rstd_ref[pl.ds(l, 1), :] + tk[:, BASE : BASE + 1]
        ).astype(BF16)
        def one_block(j, carry):
            rows = pl.ds(pl.multiple_of(j * Q_ROWS, Q_ROWS), Q_ROWS)
            scores = dot(q_ref[rows, :], kt_ref[...])
            weights = jnp.exp2(scores - jnp.max(scores, axis=1, keepdims=True)).astype(BF16)
            mixed = dot(weights, v_ref[...])
            out_ref[l, rows, :] = (mixed / mixed[:, HEAD_DIM : HEAD_DIM + 1]).astype(BF16)
            return carry
        return lax.fori_loop(0, TOKENS // Q_ROWS, one_block, carry)

    lax.fori_loop(0, count, one_latent, 0)


def attend(lat, patch, shift, scale, wq, wk, wv):
    count = lat.shape[0]
    pos = position_rows()
    centred = jnp.asarray((pos - pos.mean(axis=1, keepdims=True)).astype(np.float32))
    vmem = pl.BlockSpec(memory_space=pltpu.VMEM)
    return pl.pallas_call(
        attend_kernel,
        out_shape=jax.ShapeDtypeStruct((count, TOKENS, LANES), BF16),
        in_specs=[vmem] * 8,
        out_specs=vmem,
        scratch_shapes=[
            pltpu.VMEM((count, BASE, TOKENS), BF16),
            pltpu.VMEM((BASE, D), F32),
            pltpu.VMEM((count * ROWS, D), BF16),
            pltpu.VMEM((count * ROWS, HEAD_DIM), F32),
            pltpu.VMEM((count * ROWS, HEAD_DIM), F32),
            pltpu.VMEM((count, HEAD_DIM, ROWS), F32),
            pltpu.VMEM((LANES, TOKENS), F32),
            pltpu.VMEM((TOKENS, LANES), F32),
            pltpu.VMEM((TOKENS, HEAD_DIM), BF16),
            pltpu.VMEM((TOKENS, LANES), BF16),
            pltpu.VMEM((HEAD_DIM, TOKENS), BF16),
        ],
        cost_estimate=pl.CostEstimate(flops=8 * 10**9, bytes_accessed=4 * 10**6, transcendentals=6 * 10**6),
    )(lat, patch, centred, shift, scale, wq, wk, wv)


def shards(
    latents, timesteps, labels, guidance, keep_coef, noise_coef, w_patch, label_table,
    w_time1, w_time2, ada_weight, w_qkv, w_proj, w_fc1, w_fc2, w_out,
):
    count, tok_count, channels = latents.shape
    side = lax.axis_index("cfg")
    place = lax.axis_index("seq")
    half = w_fc2.shape[0] // 2
    fc1_half = lax.dynamic_slice_in_dim(w_fc1.T, side * half, half, 0)
    fc2_half = lax.dynamic_slice_in_dim(w_fc2, side * half, half, 0)
    proj_full = lax.all_gather(w_proj.T, "seq", axis=0, tiled=True)
    fc1_full = lax.all_gather(lax.all_gather(fc1_half, "seq", axis=0, tiled=True), "cfg", axis=0, tiled=True)
    fc2_full = lax.all_gather(lax.all_gather(fc2_half, "seq", axis=0, tiled=True), "cfg", axis=0, tiled=True)

    classes = jnp.where(side == 0, labels, CLASSES)
    steps_all = lax.all_gather(timesteps, "lat", axis=0, tiled=True)
    waves = time_waves(steps_all).astype(BF16)
    hidden_own = jax.nn.silu(dot(waves, w_time1)).astype(BF16)
    hidden_time = lax.all_gather(hidden_own, "lat", axis=1, tiled=True)
    vector_own = dot(hidden_time, w_time2)
    vector = lax.all_to_all(vector_own, "lat", split_axis=0, concat_axis=1, tiled=True)
    onehot = (classes[:, None] == jnp.arange(CLASSES + 1, dtype=jnp.int32)[None, :]).astype(BF16)
    conditioning = vector + dot(onehot, label_table)
    own_columns = dot(jax.nn.silu(conditioning).astype(BF16), ada_weight)
    modulation = lax.all_gather(own_columns, "seq", axis=1, tiled=True)
    pieces = [modulation[:, number * D : (number + 1) * D] for number in range(8)]

    lat_t = jnp.transpose(latents, (0, 2, 1)).astype(BF16)
    lat_all = lax.all_gather(lat_t, "seq", axis=2, tiled=True)
    blocks = w_qkv.T.reshape(3, HEAD_DIM, D)
    got = jnp.stack(
        [
            lax.ppermute(blocks[j], "seq", [(s, (3 * s + j) % HEADS) for s in range(HEADS)])
            for j in range(3)
        ]
    )
    head_w = [lax.dynamic_index_in_dim(got, (HEADS * kind + place) % 3, 0, False) for kind in range(3)]
    attended = attend(lat_all, w_patch, pieces[0], pieces[1], *head_w)
    arrived = lax.all_to_all(
        attended[:, :, :HEAD_DIM].reshape(count, HEADS, tok_count, HEAD_DIM), "seq", split_axis=1, concat_axis=1
    )
    attended = jnp.transpose(arrived, (0, 2, 1, 3)).reshape(count * tok_count, D)

    pos = jnp.asarray(position_rows().astype(np.float32))
    columns = pos[:GRID]
    lines = lax.dynamic_slice_in_dim(pos, GRID + place * (tok_count // GRID), tok_count // GRID, 0)
    own_pos = (columns[None] + lines[:, None]).reshape(tok_count, D)
    state = dot(latents.reshape(-1, channels).astype(BF16), w_patch).reshape(count, tok_count, D) + own_pos[None]
    projected = dot(attended, proj_full, NT).reshape(count, tok_count, D)
    state = state + pieces[2][:, None, :] * projected
    normed = (layer_norm(state) * (1.0 + pieces[4][:, None, :]) + pieces[3][:, None, :]).astype(BF16).reshape(-1, D)
    hidden = jax.nn.gelu(dot(normed, fc1_full, NT), approximate=True).astype(BF16)
    mlp_out = dot(hidden, fc2_full).reshape(count, tok_count, D)
    state = state + pieces[5][:, None, :] * mlp_out
    final = (layer_norm(state) * (1.0 + pieces[7][:, None, :]) + pieces[6][:, None, :]).astype(BF16).reshape(-1, D)
    noise_own = dot(final, w_out).reshape(count, tok_count, channels)
    half_width = channels // 2
    own_latent = lax.dynamic_slice_in_dim(latents, side * half_width, half_width, 2)
    partner = lax.ppermute(noise_own, "cfg", [(0, 1), (1, 0)])
    cond_noise = jnp.where(side == 0, noise_own, partner)
    free_noise = jnp.where(side == 0, partner, noise_own)
    combined = free_noise + guidance[0] * (cond_noise - free_noise)
    guided = lax.dynamic_slice_in_dim(combined, side * half_width, half_width, 2)
    return keep_coef[:, None, None] * own_latent + noise_coef[:, None, None] * guided


def solution(mesh):
    return jax.shard_map(
        shards,
        mesh=mesh,
        in_specs=(
            P("lat", "seq", None), P("lat"), P("lat"), P(), P("lat"), P("lat"), P(), P(),
            P(None, "lat"), P(None, "lat"), P(None, "seq"), P(None, "seq"), P(None, "seq"),
            P(None, "seq"), P("seq", None), P(),
        ),
        out_specs=P("lat", "seq", "cfg"),
        check_vma=False,
    )
```

```python
import math

import jax
import jax.numpy as jnp
import numpy as np
from jax import lax
from jax.experimental import pallas as pl
from jax.experimental.pallas import tpu as pltpu
from jax.sharding import PartitionSpec as P

D = 1152
HEADS = 16
HEAD_DIM = 72
CLASSES = 1000
FREQ = 256
GRID = 32
TOKENS = 1024
BASE = 16 + 2 * GRID
ROWS = 96
LANES = 128
Q_ROWS = 256
F32 = jnp.float32
BF16 = jnp.bfloat16
NT = (((1,), (1,)), ((), ()))
NN = (((1,), (0,)), ((), ()))
MESH = pl.DeviceIdType.MESH
HIGH = lax.Precision.HIGHEST


def position_rows():
    quarter = D // 4
    frequency = np.exp(-math.log(10000.0) * np.arange(quarter) / quarter)
    angle = np.arange(GRID)[:, None] * frequency[None, :]
    waves = np.concatenate([np.sin(angle), np.cos(angle)], axis=1)
    rows = np.zeros((2 * GRID, D))
    rows[:GRID, : D // 2] = waves
    rows[GRID:, D // 2 :] = waves
    return rows


def dot(a, b, dims=NN, precision=None):
    return lax.dot_general(a, b, dims, precision=precision, preferred_element_type=F32)


def layer_norm(values):
    average = jnp.mean(values, axis=-1, keepdims=True)
    centered = values - average
    spread = jnp.mean(centered * centered, axis=-1, keepdims=True)
    return centered * lax.rsqrt(spread + 1e-06)


def time_waves(timesteps):
    half_count = FREQ // 2
    frequency = jnp.exp(-math.log(10000.0) * jnp.arange(half_count, dtype=F32) / half_count)
    angles = timesteps.astype(F32)[:, None] * frequency[None, :]
    return jnp.concatenate([jnp.cos(angles), jnp.sin(angles)], axis=-1)


def attend_kernel(
    lat_ref, patch_ref, pos_ref, shift_ref, scale_ref, wq_ref, wk_ref, wv_ref,
    out_ref, ft_ref, base_ref, xs_ref, tq_ref, tv_ref, tk_ref, rstd_ref, rcol_ref, q_ref, v_ref, kt_ref,
):
    count = lat_ref.shape[0]
    patch = patch_ref[...].astype(F32)
    base_ref[:16, :] = patch - jnp.mean(patch, axis=1, keepdims=True)
    base_ref[16:, :] = pos_ref[...]
    base = base_ref[...]
    gram = dot(base, base, NT, HIGH) * (1.0 / D)
    token = lax.broadcasted_iota(jnp.int32, (2 * GRID, TOKENS), 1)
    place = lax.broadcasted_iota(jnp.int32, (2 * GRID, TOKENS), 0)
    hot = jnp.where(jnp.where(place < GRID, token % GRID, token // GRID + GRID) == place, 1.0, 0.0).astype(BF16)
    rstd_ref[...] = jnp.zeros_like(rstd_ref)
    for l in range(count):
        ft_ref[l, :16, :] = lat_ref[l]
        ft_ref[l, 16:, :] = hot
        ft = ft_ref[l].astype(F32)
        spread = jnp.sum(dot(gram, ft, NN, HIGH) * ft, axis=0, keepdims=True)
        rstd_ref[l : l + 1, :] = lax.rsqrt(spread + 1e-06)
        xs_ref[l * ROWS : l * ROWS + BASE, :] = (base * (1.0 + scale_ref[l : l + 1, :])).astype(BF16)
        xs_ref[l * ROWS + BASE : (l + 1) * ROWS, :] = jnp.broadcast_to(
            shift_ref[l : l + 1, :], (ROWS - BASE, D)
        ).astype(BF16)
    rcol_ref[...] = jnp.transpose(rstd_ref[...])
    factor = math.log2(math.e) / math.sqrt(HEAD_DIM)
    tq_ref[...] = dot(xs_ref[...], wq_ref[...], NT) * factor
    tv_ref[...] = dot(xs_ref[...], wv_ref[...], NT)
    for l in range(count):
        tk_ref[l] = dot(wk_ref[...], xs_ref[l * ROWS : (l + 1) * ROWS, :], NT)
    ones_lane = lax.broadcasted_iota(jnp.int32, (TOKENS, LANES), 1) == HEAD_DIM
    v_ref[...] = jnp.where(ones_lane, 1.0, 0.0).astype(BF16)

    def one_latent(l, carry):
        ft = ft_ref[l]
        f = jnp.transpose(ft.astype(F32)).astype(BF16)
        lane = lax.broadcasted_iota(jnp.int32, (TOKENS, LANES), 1)
        column = jnp.sum(jnp.where(lane == l, rcol_ref[...], 0.0), axis=1, keepdims=True)
        top = pl.multiple_of(l * ROWS, ROWS)
        tq = tq_ref[pl.ds(top, ROWS), :]
        tv = tv_ref[pl.ds(top, ROWS), :]
        tk = tk_ref[l]
        q_ref[...] = (dot(f, tq[:BASE].astype(BF16)) * column + tq[BASE : BASE + 1]).astype(BF16)
        v_ref[:, :HEAD_DIM] = (dot(f, tv[:BASE].astype(BF16)) * column + tv[BASE : BASE + 1]).astype(BF16)
        kt_ref[...] = (
            dot(tk[:, :BASE].astype(BF16), ft) * rstd_ref[pl.ds(l, 1), :] + tk[:, BASE : BASE + 1]
        ).astype(BF16)
        def one_block(j, carry):
            rows = pl.ds(pl.multiple_of(j * Q_ROWS, Q_ROWS), Q_ROWS)
            scores = dot(q_ref[rows, :], kt_ref[...])
            weights = jnp.exp2(scores - jnp.max(scores, axis=1, keepdims=True)).astype(BF16)
            mixed = dot(weights, v_ref[...])
            out_ref[l, rows, :] = (mixed / mixed[:, HEAD_DIM : HEAD_DIM + 1]).astype(BF16)
            return carry
        return lax.fori_loop(0, TOKENS // Q_ROWS, one_block, carry)

    lax.fori_loop(0, count, one_latent, 0)


def attend(lat, patch, shift, scale, wq, wk, wv):
    count = lat.shape[0]
    pos = position_rows()
    centred = jnp.asarray((pos - pos.mean(axis=1, keepdims=True)).astype(np.float32))
    vmem = pl.BlockSpec(memory_space=pltpu.VMEM)
    return pl.pallas_call(
        attend_kernel,
        out_shape=jax.ShapeDtypeStruct((count, TOKENS, LANES), BF16),
        in_specs=[vmem] * 8,
        out_specs=vmem,
        scratch_shapes=[
            pltpu.VMEM((count, BASE, TOKENS), BF16),
            pltpu.VMEM((BASE, D), F32),
            pltpu.VMEM((count * ROWS, D), BF16),
            pltpu.VMEM((count * ROWS, HEAD_DIM), F32),
            pltpu.VMEM((count * ROWS, HEAD_DIM), F32),
            pltpu.VMEM((count, HEAD_DIM, ROWS), F32),
            pltpu.VMEM((LANES, TOKENS), F32),
            pltpu.VMEM((TOKENS, LANES), F32),
            pltpu.VMEM((TOKENS, HEAD_DIM), BF16),
            pltpu.VMEM((TOKENS, LANES), BF16),
            pltpu.VMEM((HEAD_DIM, TOKENS), BF16),
        ],
        cost_estimate=pl.CostEstimate(flops=8 * 10**9, bytes_accessed=4 * 10**6, transcendentals=6 * 10**6),
    )(lat, patch, centred, shift, scale, wq, wk, wv)


def feed_forward_kernel(
    guidance_ref, state_ref, shift_ref, scale_ref, gate_ref, last_shift_ref, last_scale_ref, fc1_ref, fc2_ref, out_w_ref,
    out_ref, normed_ref, total_ref, noise_ref, partner_ref, send_sem, recv_sem,
):
    step = pl.program_id(0)
    side = lax.axis_index("cfg")
    count = shift_ref.shape[0]
    tokens = state_ref.shape[0] // count
    barrier = pltpu.get_barrier_semaphore()

    @pl.when(step == 0)
    def _():
        pl.semaphore_signal(barrier, inc=1, device_id={"cfg": 1 - side}, device_id_type=MESH)
        for l in range(count):
            rows = slice(l * tokens, (l + 1) * tokens)
            normed_ref[rows, :] = (
                layer_norm(state_ref[rows, :]) * (1.0 + scale_ref[l : l + 1, :]) + shift_ref[l : l + 1, :]
            ).astype(BF16)
        total_ref[...] = jnp.zeros_like(total_ref)

    units = fc1_ref.shape[0] * fc1_ref.shape[1]
    hidden = dot(normed_ref[...], fc1_ref[...].reshape(units, D), NT)
    hidden = jax.nn.gelu(hidden, approximate=True).astype(BF16)
    total_ref[...] += dot(hidden, fc2_ref[...].reshape(units, D))

    @pl.when(step == pl.num_programs(0) - 1)
    def _():
        for l in range(count):
            rows = slice(l * tokens, (l + 1) * tokens)
            state = state_ref[rows, :] + gate_ref[l : l + 1, :] * total_ref[rows, :]
            normed_ref[rows, :] = (
                layer_norm(state) * (1.0 + last_scale_ref[l : l + 1, :]) + last_shift_ref[l : l + 1, :]
            ).astype(BF16)
        noise_ref[...] = dot(out_w_ref[...], normed_ref[...], (((0,), (1,)), ((), ())))
        pl.semaphore_wait(barrier, 1)
        copy = pltpu.make_async_remote_copy(
            src_ref=noise_ref.at[pl.ds(pl.multiple_of((1 - side) * 8, 8), 8)],
            dst_ref=partner_ref,
            send_sem=send_sem,
            recv_sem=recv_sem,
            device_id={"cfg": 1 - side},
            device_id_type=MESH,
        )
        copy.start()
        copy.wait()
        own = noise_ref[pl.ds(pl.multiple_of(side * 8, 8), 8), :]
        cond_noise = jnp.where(side == 0, own, partner_ref[...])
        free_noise = jnp.where(side == 0, partner_ref[...], own)
        out_ref[...] = free_noise + guidance_ref[0] * (cond_noise - free_noise)


def feed_forward(state, pieces, stacked, w_out, guidance, rows):
    tokens = state.shape[0]
    shift, scale, gate, last_shift, last_scale = pieces
    whole = pl.BlockSpec(memory_space=pltpu.VMEM)
    group = 4
    weights = [pl.BlockSpec((group, rows, D), lambda i, b=b: (i, b, 0)) for b in range(2)]
    return pl.pallas_call(
        feed_forward_kernel,
        grid=(stacked.shape[0] // group,),
        out_shape=jax.ShapeDtypeStruct((8, tokens), F32),
        in_specs=[pl.BlockSpec(memory_space=pltpu.SMEM)] + [whole] * 6 + weights + [whole],
        out_specs=whole,
        scratch_shapes=[
            pltpu.VMEM((tokens, D), BF16),
            pltpu.VMEM((tokens, D), F32),
            pltpu.VMEM((16, tokens), F32),
            pltpu.VMEM((8, tokens), F32),
            pltpu.SemaphoreType.DMA,
            pltpu.SemaphoreType.DMA,
        ],
        compiler_params=pltpu.CompilerParams(collective_id=0, has_side_effects=True),
        cost_estimate=pl.CostEstimate(flops=8 * 10**9, bytes_accessed=24 * 10**6, transcendentals=2 * 10**6),
    )(guidance, state, shift, scale, gate, last_shift, last_scale, stacked, stacked, w_out)


def shards(
    latents, timesteps, labels, guidance, keep_coef, noise_coef, w_patch, label_table,
    w_time1, w_time2, ada_weight, w_qkv, w_proj, w_fc1, w_fc2, w_out,
):
    count, tok_count, channels = latents.shape
    side = lax.axis_index("cfg")
    place = lax.axis_index("seq")
    rows = w_fc2.shape[0]
    stacked = lax.all_gather(jnp.concatenate([w_fc1.T, w_fc2, w_proj.T], axis=0), "seq", axis=0)
    proj_full = stacked[:, 2 * rows :].reshape(D, D)

    classes = jnp.where(side == 0, labels, CLASSES)
    steps_all = lax.all_gather(timesteps, "lat", axis=0, tiled=True)
    waves = time_waves(steps_all).astype(BF16)
    hidden_own = jax.nn.silu(dot(waves, w_time1)).astype(BF16)
    hidden_time = lax.all_gather(hidden_own, "lat", axis=1, tiled=True)
    vector_own = dot(hidden_time, w_time2)
    vector = lax.all_to_all(vector_own, "lat", split_axis=0, concat_axis=1, tiled=True)
    onehot = (classes[:, None] == jnp.arange(CLASSES + 1, dtype=jnp.int32)[None, :]).astype(BF16)
    conditioning = vector + dot(onehot, label_table)
    own_columns = dot(jax.nn.silu(conditioning).astype(BF16), ada_weight)
    modulation = lax.all_gather(own_columns, "seq", axis=1, tiled=True)
    pieces = [modulation[:, number * D : (number + 1) * D] for number in range(8)]

    lat_t = jnp.transpose(latents, (0, 2, 1)).astype(BF16)
    lat_all = lax.all_gather(lat_t, "seq", axis=2, tiled=True)
    blocks = w_qkv.T.reshape(3, HEAD_DIM, D)
    got = jnp.stack(
        [
            lax.ppermute(blocks[j], "seq", [(s, (3 * s + j) % HEADS) for s in range(HEADS)])
            for j in range(3)
        ]
    )
    head_w = [lax.dynamic_index_in_dim(got, (HEADS * kind + place) % 3, 0, False) for kind in range(3)]
    attended = attend(lat_all, w_patch, pieces[0], pieces[1], *head_w)
    arrived = lax.all_to_all(
        attended[:, :, :HEAD_DIM].reshape(count, HEADS, tok_count, HEAD_DIM), "seq", split_axis=1, concat_axis=1
    )
    attended = jnp.transpose(arrived, (0, 2, 1, 3)).reshape(count * tok_count, D)

    pos = jnp.asarray(position_rows().astype(np.float32))
    columns = pos[:GRID]
    lines = lax.dynamic_slice_in_dim(pos, GRID + place * (tok_count // GRID), tok_count // GRID, 0)
    own_pos = (columns[None] + lines[:, None]).reshape(tok_count, D)
    state = dot(latents.reshape(-1, channels).astype(BF16), w_patch).reshape(count, tok_count, D) + own_pos[None]
    projected = dot(attended, proj_full, NT).reshape(count, tok_count, D)
    state = state + pieces[2][:, None, :] * projected
    guided = feed_forward(state.reshape(-1, D), pieces[3:], stacked, w_out, guidance, rows)
    half_width = channels // 2
    own_latent = lax.dynamic_slice_in_dim(latents, side * half_width, half_width, 2)
    guided = guided.T.reshape(count, tok_count, half_width)
    return keep_coef[:, None, None] * own_latent + noise_coef[:, None, None] * guided


def solution(mesh):
    return jax.shard_map(
        shards,
        mesh=mesh,
        in_specs=(
            P("lat", "seq", None), P("lat"), P("lat"), P(), P("lat"), P("lat"), P(), P(),
            P(None, "lat"), P(None, "lat"), P(None, "seq"), P(None, "seq"), P(None, "seq"),
            P(None, "seq"), P("seq", None), P(),
        ),
        out_specs=P("lat", "seq", "cfg"),
        check_vma=False,
    )
```

```python
import math

import jax
import jax.numpy as jnp
import numpy as np
from jax import lax
from jax.experimental import pallas as pl
from jax.experimental.pallas import tpu as pltpu
from jax.sharding import PartitionSpec as P

D = 1152
HEADS = 16
HEAD_DIM = 72
CLASSES = 1000
FREQ = 256
GRID = 32
TOKENS = 1024
BASE = 16 + 2 * GRID
ROWS = 96
LANES = 128
Q_ROWS = 256
F32 = jnp.float32
BF16 = jnp.bfloat16
NT = (((1,), (1,)), ((), ()))
NN = (((1,), (0,)), ((), ()))
MESH = pl.DeviceIdType.MESH
HIGH = lax.Precision.HIGHEST


def position_rows():
    quarter = D // 4
    frequency = np.exp(-math.log(10000.0) * np.arange(quarter) / quarter)
    angle = np.arange(GRID)[:, None] * frequency[None, :]
    waves = np.concatenate([np.sin(angle), np.cos(angle)], axis=1)
    rows = np.zeros((2 * GRID, D))
    rows[:GRID, : D // 2] = waves
    rows[GRID:, D // 2 :] = waves
    return rows


def dot(a, b, dims=NN, precision=None):
    return lax.dot_general(a, b, dims, precision=precision, preferred_element_type=F32)


def layer_norm(values):
    average = jnp.mean(values, axis=-1, keepdims=True)
    centered = values - average
    spread = jnp.mean(centered * centered, axis=-1, keepdims=True)
    return centered * lax.rsqrt(spread + 1e-06)


def time_waves(timesteps):
    half_count = FREQ // 2
    frequency = jnp.exp(-math.log(10000.0) * jnp.arange(half_count, dtype=F32) / half_count)
    angles = timesteps.astype(F32)[:, None] * frequency[None, :]
    return jnp.concatenate([jnp.cos(angles), jnp.sin(angles)], axis=-1)


def ring(me, body):
    def one(k, carry):
        body(k, lax.rem(me + k, HEADS))
        return carry

    lax.fori_loop(1, HEADS, one, 0)


def remote(source, target, send_sem, recv_sem, peer):
    return pltpu.make_async_remote_copy(
        src_ref=source, dst_ref=target, send_sem=send_sem, recv_sem=recv_sem, device_id=peer, device_id_type=MESH
    )


def attend_kernel(
    lat_ref, cols_ref, patch_ref, pos_ref, wq_ref, wk_ref, wv_ref,
    out_ref, mods_ref,
    lat_all, cols_all, arrived, own_ref, lat_send, lat_recv, cols_send, cols_recv, out_send, out_recv,
    ft_ref, base_ref, xs_ref, tq_ref, tv_ref, tk_ref, rstd_ref, rcol_ref, q_ref, v_ref, kt_ref,
):
    count = lat_ref.shape[0]
    tokens = lat_ref.shape[2]
    me = lax.axis_index("seq")
    barrier = pltpu.get_barrier_semaphore()
    ring(me, lambda k, peer: pl.semaphore_signal(barrier, inc=1, device_id={"seq": peer}, device_id_type=MESH))
    pl.semaphore_wait(barrier, HEADS - 1)

    def send_inputs(k, peer):
        remote(cols_ref, cols_all.at[me], cols_send.at[k], cols_recv.at[me], {"seq": peer}).start()
        remote(lat_ref, lat_all.at[me], lat_send.at[k], lat_recv.at[me], {"seq": peer}).start()

    def wait_inputs(k, peer):
        remote(cols_ref, cols_all.at[peer], cols_send.at[k], cols_recv.at[peer], {"seq": peer}).wait()
        remote(lat_ref, lat_all.at[peer], lat_send.at[k], lat_recv.at[peer], {"seq": peer}).wait()

    ring(me, send_inputs)
    lat_all[me] = lat_ref[...]
    cols_all[me] = cols_ref[...]
    patch = patch_ref[...].astype(F32)
    base_ref[:16, :] = patch - jnp.mean(patch, axis=1, keepdims=True)
    base_ref[16:, :] = pos_ref[...]
    base = base_ref[...]
    gram = dot(base, base, NT, HIGH) * (1.0 / D)
    token = lax.broadcasted_iota(jnp.int32, (2 * GRID, TOKENS), 1)
    place = lax.broadcasted_iota(jnp.int32, (2 * GRID, TOKENS), 0)
    hot = jnp.where(jnp.where(place < GRID, token % GRID, token // GRID + GRID) == place, 1.0, 0.0).astype(BF16)
    rstd_ref[...] = jnp.zeros_like(rstd_ref)
    ring(me, wait_inputs)
    for n in range(8):
        mods_ref[n] = jnp.concatenate([cols_all[2 * n], cols_all[2 * n + 1]], axis=1)
    for l in range(count):
        for n in range(HEADS // 2):
            pair = [lat_all[2 * n + m, l].astype(F32) for m in range(2)]
            ft_ref[l, :16, n * LANES : (n + 1) * LANES] = jnp.concatenate(pair, axis=1).astype(BF16)
        ft_ref[l, 16:, :] = hot
        ft = ft_ref[l].astype(F32)
        spread = jnp.sum(dot(gram, ft, NN, HIGH) * ft, axis=0, keepdims=True)
        rstd_ref[l : l + 1, :] = lax.rsqrt(spread + 1e-06)
        xs_ref[l * ROWS : l * ROWS + BASE, :] = (base * (1.0 + mods_ref[1, l : l + 1, :])).astype(BF16)
        xs_ref[l * ROWS + BASE : (l + 1) * ROWS, :] = jnp.broadcast_to(
            mods_ref[0, l : l + 1, :], (ROWS - BASE, D)
        ).astype(BF16)
    rcol_ref[...] = jnp.transpose(rstd_ref[...])
    factor = math.log2(math.e) / math.sqrt(HEAD_DIM)
    tq_ref[...] = dot(xs_ref[...], wq_ref[...], NT) * factor
    tv_ref[...] = dot(xs_ref[...], wv_ref[...], NT)
    for l in range(count):
        tk_ref[l] = dot(wk_ref[...], xs_ref[l * ROWS : (l + 1) * ROWS, :], NT)
    ones_lane = lax.broadcasted_iota(jnp.int32, (TOKENS, LANES), 1) == HEAD_DIM
    v_ref[...] = jnp.where(ones_lane, 1.0, 0.0).astype(BF16)

    def one_latent(l, carry):
        ft = ft_ref[l]
        f = jnp.transpose(ft.astype(F32)).astype(BF16)
        lane = lax.broadcasted_iota(jnp.int32, (TOKENS, LANES), 1)
        column = jnp.sum(jnp.where(lane == l, rcol_ref[...], 0.0), axis=1, keepdims=True)
        top = pl.multiple_of(l * ROWS, ROWS)
        tq = tq_ref[pl.ds(top, ROWS), :]
        tv = tv_ref[pl.ds(top, ROWS), :]
        tk = tk_ref[l]
        q_ref[...] = (dot(f, tq[:BASE].astype(BF16)) * column + tq[BASE : BASE + 1]).astype(BF16)
        v_ref[:, :HEAD_DIM] = (dot(f, tv[:BASE].astype(BF16)) * column + tv[BASE : BASE + 1]).astype(BF16)
        kt_ref[...] = (
            dot(tk[:, :BASE].astype(BF16), ft) * rstd_ref[pl.ds(l, 1), :] + tk[:, BASE : BASE + 1]
        ).astype(BF16)
        def one_block(j, carry):
            rows = pl.ds(pl.multiple_of(j * Q_ROWS, Q_ROWS), Q_ROWS)
            scores = dot(q_ref[rows, :], kt_ref[...])
            weights = jnp.exp2(scores - jnp.max(scores, axis=1, keepdims=True)).astype(BF16)
            mixed = dot(weights, v_ref[...])
            own_ref[l, rows, :] = (mixed / mixed[:, HEAD_DIM : HEAD_DIM + 1]).astype(BF16)
            return carry
        lax.fori_loop(0, TOKENS // Q_ROWS, one_block, 0)
        ring(me, lambda k, peer: send_out(l, k, peer).start())
        arrived[me, l] = own_ref[l, rows_of(me), :]
        return carry

    def rows_of(peer):
        return pl.ds(pl.multiple_of(peer * tokens, tokens), tokens)

    def send_out(l, k, peer):
        return remote(
            own_ref.at[l, rows_of(peer)], arrived.at[me, l], out_send.at[k, l], out_recv.at[me, l], {"seq": peer}
        )

    def wait_out(k, peer):
        def one(l, carry):
            remote(
                own_ref.at[l, rows_of(peer)], arrived.at[peer, l], out_send.at[k, l], out_recv.at[peer, l], {"seq": peer}
            ).wait()
            return carry

        lax.fori_loop(0, count, one, 0)

    lax.fori_loop(0, count, one_latent, 0)
    ring(me, wait_out)
    for l in range(count):
        heads = [arrived[h, l].astype(F32)[:, :HEAD_DIM] for h in range(HEADS)]
        out_ref[l * tokens : (l + 1) * tokens, :] = jnp.concatenate(heads, axis=1).astype(BF16)


def attend(lat, cols, patch, wq, wk, wv):
    count, channels, tokens = lat.shape
    pos = position_rows()
    centred = jnp.asarray((pos - pos.mean(axis=1, keepdims=True)).astype(np.float32))
    vmem = pl.BlockSpec(memory_space=pltpu.VMEM)
    return pl.pallas_call(
        attend_kernel,
        out_shape=(jax.ShapeDtypeStruct((count * tokens, D), BF16), jax.ShapeDtypeStruct((8, count, D), F32)),
        in_specs=[vmem] * 7,
        out_specs=(vmem, vmem),
        scratch_shapes=[
            pltpu.VMEM((HEADS, count, channels, tokens), BF16),
            pltpu.VMEM((HEADS,) + cols.shape, F32),
            pltpu.VMEM((HEADS, count, tokens, LANES), BF16),
            pltpu.VMEM((count, TOKENS, LANES), BF16),
        ]
        + [pltpu.SemaphoreType.DMA((HEADS,))] * 4
        + [pltpu.SemaphoreType.DMA((HEADS, count))] * 2
        + [
            pltpu.VMEM((count, BASE, TOKENS), BF16),
            pltpu.VMEM((BASE, D), F32),
            pltpu.VMEM((count * ROWS, D), BF16),
            pltpu.VMEM((count * ROWS, HEAD_DIM), F32),
            pltpu.VMEM((count * ROWS, HEAD_DIM), F32),
            pltpu.VMEM((count, HEAD_DIM, ROWS), F32),
            pltpu.VMEM((LANES, TOKENS), F32),
            pltpu.VMEM((TOKENS, LANES), F32),
            pltpu.VMEM((TOKENS, HEAD_DIM), BF16),
            pltpu.VMEM((TOKENS, LANES), BF16),
            pltpu.VMEM((HEAD_DIM, TOKENS), BF16),
        ],
        compiler_params=pltpu.CompilerParams(collective_id=1, has_side_effects=True),
        cost_estimate=pl.CostEstimate(flops=8 * 10**9, bytes_accessed=4 * 10**6, transcendentals=6 * 10**6),
    )(lat, cols, patch, centred, wq, wk, wv)


def feed_forward_kernel(
    guidance_ref, state_ref, shift_ref, scale_ref, gate_ref, last_shift_ref, last_scale_ref, fc1_ref, fc2_ref, out_w_ref,
    out_ref, normed_ref, total_ref, noise_ref, partner_ref, send_sem, recv_sem,
):
    step = pl.program_id(0)
    side = lax.axis_index("cfg")
    count = shift_ref.shape[0]
    tokens = state_ref.shape[0] // count
    barrier = pltpu.get_barrier_semaphore()

    @pl.when(step == 0)
    def _():
        pl.semaphore_signal(barrier, inc=1, device_id={"cfg": 1 - side}, device_id_type=MESH)
        for l in range(count):
            rows = slice(l * tokens, (l + 1) * tokens)
            normed_ref[rows, :] = (
                layer_norm(state_ref[rows, :]) * (1.0 + scale_ref[l : l + 1, :]) + shift_ref[l : l + 1, :]
            ).astype(BF16)
        total_ref[...] = jnp.zeros_like(total_ref)

    units = fc1_ref.shape[0] * fc1_ref.shape[1]
    hidden = dot(normed_ref[...], fc1_ref[...].reshape(units, D), NT)
    hidden = jax.nn.gelu(hidden, approximate=True).astype(BF16)
    total_ref[...] += dot(hidden, fc2_ref[...].reshape(units, D))

    @pl.when(step == pl.num_programs(0) - 1)
    def _():
        for l in range(count):
            rows = slice(l * tokens, (l + 1) * tokens)
            state = state_ref[rows, :] + gate_ref[l : l + 1, :] * total_ref[rows, :]
            normed_ref[rows, :] = (
                layer_norm(state) * (1.0 + last_scale_ref[l : l + 1, :]) + last_shift_ref[l : l + 1, :]
            ).astype(BF16)
        noise_ref[...] = dot(out_w_ref[...], normed_ref[...], (((0,), (1,)), ((), ())))
        pl.semaphore_wait(barrier, 1)
        copy = pltpu.make_async_remote_copy(
            src_ref=noise_ref.at[pl.ds(pl.multiple_of((1 - side) * 8, 8), 8)],
            dst_ref=partner_ref,
            send_sem=send_sem,
            recv_sem=recv_sem,
            device_id={"cfg": 1 - side},
            device_id_type=MESH,
        )
        copy.start()
        copy.wait()
        own = noise_ref[pl.ds(pl.multiple_of(side * 8, 8), 8), :]
        cond_noise = jnp.where(side == 0, own, partner_ref[...])
        free_noise = jnp.where(side == 0, partner_ref[...], own)
        out_ref[...] = free_noise + guidance_ref[0] * (cond_noise - free_noise)


def feed_forward(state, pieces, stacked, w_out, guidance, rows):
    tokens = state.shape[0]
    shift, scale, gate, last_shift, last_scale = pieces
    whole = pl.BlockSpec(memory_space=pltpu.VMEM)
    group = 4
    weights = [pl.BlockSpec((group, rows, D), lambda i, b=b: (i, b, 0)) for b in range(2)]
    return pl.pallas_call(
        feed_forward_kernel,
        grid=(stacked.shape[0] // group,),
        out_shape=jax.ShapeDtypeStruct((8, tokens), F32),
        in_specs=[pl.BlockSpec(memory_space=pltpu.SMEM)] + [whole] * 6 + weights + [whole],
        out_specs=whole,
        scratch_shapes=[
            pltpu.VMEM((tokens, D), BF16),
            pltpu.VMEM((tokens, D), F32),
            pltpu.VMEM((16, tokens), F32),
            pltpu.VMEM((8, tokens), F32),
            pltpu.SemaphoreType.DMA,
            pltpu.SemaphoreType.DMA,
        ],
        compiler_params=pltpu.CompilerParams(collective_id=0, has_side_effects=True),
        cost_estimate=pl.CostEstimate(flops=8 * 10**9, bytes_accessed=24 * 10**6, transcendentals=2 * 10**6),
    )(guidance, state, shift, scale, gate, last_shift, last_scale, stacked, stacked, w_out)


def shards(
    latents, timesteps, labels, guidance, keep_coef, noise_coef, w_patch, label_table,
    w_time1, w_time2, ada_weight, w_qkv, w_proj, w_fc1, w_fc2, w_out,
):
    count, tok_count, channels = latents.shape
    side = lax.axis_index("cfg")
    place = lax.axis_index("seq")
    rows = w_fc2.shape[0]
    stacked = lax.all_gather(jnp.concatenate([w_fc1.T, w_fc2, w_proj.T], axis=0), "seq", axis=0)
    proj_full = stacked[:, 2 * rows :].reshape(D, D)

    classes = jnp.where(side == 0, labels, CLASSES)
    steps_all = lax.all_gather(timesteps, "lat", axis=0, tiled=True)
    waves = time_waves(steps_all).astype(BF16)
    hidden_own = jax.nn.silu(dot(waves, w_time1)).astype(BF16)
    hidden_time = lax.all_gather(hidden_own, "lat", axis=1, tiled=True)
    vector_own = dot(hidden_time, w_time2)
    vector = lax.all_to_all(vector_own, "lat", split_axis=0, concat_axis=1, tiled=True)
    onehot = (classes[:, None] == jnp.arange(CLASSES + 1, dtype=jnp.int32)[None, :]).astype(BF16)
    conditioning = vector + dot(onehot, label_table)
    own_columns = dot(jax.nn.silu(conditioning).astype(BF16), ada_weight)
    lat_t = jnp.transpose(latents, (0, 2, 1)).astype(BF16)
    blocks = w_qkv.T.reshape(3, HEAD_DIM, D)
    got = jnp.stack(
        [
            lax.ppermute(blocks[j], "seq", [(s, (3 * s + j) % HEADS) for s in range(HEADS)])
            for j in range(3)
        ]
    )
    head_w = [lax.dynamic_index_in_dim(got, (HEADS * kind + place) % 3, 0, False) for kind in range(3)]
    attended, mods = attend(lat_t, own_columns, w_patch, *head_w)
    pieces = [mods[n] for n in range(8)]

    pos = jnp.asarray(position_rows().astype(np.float32))
    columns = pos[:GRID]
    lines = lax.dynamic_slice_in_dim(pos, GRID + place * (tok_count // GRID), tok_count // GRID, 0)
    own_pos = (columns[None] + lines[:, None]).reshape(tok_count, D)
    state = dot(latents.reshape(-1, channels).astype(BF16), w_patch).reshape(count, tok_count, D) + own_pos[None]
    projected = dot(attended, proj_full, NT).reshape(count, tok_count, D)
    state = state + pieces[2][:, None, :] * projected
    guided = feed_forward(state.reshape(-1, D), pieces[3:], stacked, w_out, guidance, rows)
    half_width = channels // 2
    own_latent = lax.dynamic_slice_in_dim(latents, side * half_width, half_width, 2)
    guided = guided.T.reshape(count, tok_count, half_width)
    return keep_coef[:, None, None] * own_latent + noise_coef[:, None, None] * guided


def solution(mesh):
    return jax.shard_map(
        shards,
        mesh=mesh,
        in_specs=(
            P("lat", "seq", None), P("lat"), P("lat"), P(), P("lat"), P("lat"), P(), P(),
            P(None, "lat"), P(None, "lat"), P(None, "seq"), P(None, "seq"), P(None, "seq"),
            P(None, "seq"), P("seq", None), P(),
        ),
        out_specs=P("lat", "seq", "cfg"),
        check_vma=False,
    )
```

```python
import math

import jax
import jax.numpy as jnp
import numpy as np
from jax import lax
from jax.experimental import pallas as pl
from jax.experimental.pallas import tpu as pltpu
from jax.sharding import PartitionSpec as P

D = 1152
HEADS = 16
HEAD_DIM = 72
CLASSES = 1000
FREQ = 256
GRID = 32
TOKENS = 1024
BASE = 16 + 2 * GRID
ROWS = 96
LANES = 128
Q_ROWS = 256
F32 = jnp.float32
BF16 = jnp.bfloat16
NT = (((1,), (1,)), ((), ()))
NN = (((1,), (0,)), ((), ()))
MESH = pl.DeviceIdType.MESH
HIGH = lax.Precision.HIGHEST


def position_rows():
    quarter = D // 4
    frequency = np.exp(-math.log(10000.0) * np.arange(quarter) / quarter)
    angle = np.arange(GRID)[:, None] * frequency[None, :]
    waves = np.concatenate([np.sin(angle), np.cos(angle)], axis=1)
    rows = np.zeros((2 * GRID, D))
    rows[:GRID, : D // 2] = waves
    rows[GRID:, D // 2 :] = waves
    return rows


def dot(a, b, dims=NN, precision=None):
    return lax.dot_general(a, b, dims, precision=precision, preferred_element_type=F32)


def layer_norm(values):
    average = jnp.mean(values, axis=-1, keepdims=True)
    centered = values - average
    spread = jnp.mean(centered * centered, axis=-1, keepdims=True)
    return centered * lax.rsqrt(spread + 1e-06)


def time_waves(timesteps):
    half_count = FREQ // 2
    frequency = jnp.exp(-math.log(10000.0) * jnp.arange(half_count, dtype=F32) / half_count)
    angles = timesteps.astype(F32)[:, None] * frequency[None, :]
    return jnp.concatenate([jnp.cos(angles), jnp.sin(angles)], axis=-1)


def ring(me, body):
    def one(k, carry):
        body(k, lax.rem(me + k, HEADS))
        return carry

    lax.fori_loop(1, HEADS, one, 0)


def remote(source, target, send_sem, recv_sem, peer):
    return pltpu.make_async_remote_copy(
        src_ref=source, dst_ref=target, send_sem=send_sem, recv_sem=recv_sem, device_id=peer, device_id_type=MESH
    )


def attend_kernel(
    lat_ref, cols_ref, patch_ref, pos_ref, wq_ref, wk_ref, wv_ref,
    out_ref, mods_ref,
    lat_all, cols_all, arrived, own_ref, lat_send, lat_recv, cols_send, cols_recv, out_send, out_recv,
    ft_ref, base_ref, xs_ref, tq_ref, tv_ref, tk_ref, rstd_ref, rcol_ref, q_ref, v_ref, kt_ref,
):
    count = lat_ref.shape[0]
    tokens = lat_ref.shape[2]
    me = lax.axis_index("seq")
    barrier = pltpu.get_barrier_semaphore()
    ring(me, lambda k, peer: pl.semaphore_signal(barrier, inc=1, device_id={"seq": peer}, device_id_type=MESH))
    pl.semaphore_wait(barrier, HEADS - 1)

    def send_inputs(k, peer):
        remote(cols_ref, cols_all.at[me], cols_send.at[k], cols_recv.at[me], {"seq": peer}).start()
        remote(lat_ref, lat_all.at[me], lat_send.at[k], lat_recv.at[me], {"seq": peer}).start()

    def wait_inputs(k, peer):
        remote(cols_ref, cols_all.at[peer], cols_send.at[k], cols_recv.at[peer], {"seq": peer}).wait()
        remote(lat_ref, lat_all.at[peer], lat_send.at[k], lat_recv.at[peer], {"seq": peer}).wait()

    ring(me, send_inputs)
    lat_all[me] = lat_ref[...]
    cols_all[me] = cols_ref[...]
    patch = patch_ref[...].astype(F32)
    base_ref[:16, :] = patch - jnp.mean(patch, axis=1, keepdims=True)
    base_ref[16:, :] = pos_ref[...]
    base = base_ref[...]
    gram = dot(base, base, NT, HIGH) * (1.0 / D)
    token = lax.broadcasted_iota(jnp.int32, (2 * GRID, TOKENS), 1)
    place = lax.broadcasted_iota(jnp.int32, (2 * GRID, TOKENS), 0)
    hot = jnp.where(jnp.where(place < GRID, token % GRID, token // GRID + GRID) == place, 1.0, 0.0).astype(BF16)
    rstd_ref[...] = jnp.zeros_like(rstd_ref)
    ring(me, wait_inputs)
    for n in range(8):
        mods_ref[n] = jnp.concatenate([cols_all[2 * n], cols_all[2 * n + 1]], axis=1)
    for l in range(count):
        for n in range(HEADS // 2):
            pair = [lat_all[2 * n + m, l].astype(F32) for m in range(2)]
            ft_ref[l, :16, n * LANES : (n + 1) * LANES] = jnp.concatenate(pair, axis=1).astype(BF16)
        ft_ref[l, 16:, :] = hot
        ft = ft_ref[l].astype(F32)
        spread = jnp.sum(dot(gram, ft, NN, HIGH) * ft, axis=0, keepdims=True)
        rstd_ref[l : l + 1, :] = lax.rsqrt(spread + 1e-06)
        xs_ref[l * ROWS : l * ROWS + BASE, :] = (base * (1.0 + mods_ref[1, l : l + 1, :])).astype(BF16)
        xs_ref[l * ROWS + BASE : (l + 1) * ROWS, :] = jnp.broadcast_to(
            mods_ref[0, l : l + 1, :], (ROWS - BASE, D)
        ).astype(BF16)
    rcol_ref[...] = jnp.transpose(rstd_ref[...])
    factor = math.log2(math.e) / math.sqrt(HEAD_DIM)
    tq_ref[...] = dot(xs_ref[...], wq_ref[...], NT) * factor
    tv_ref[...] = dot(xs_ref[...], wv_ref[...], NT)
    for l in range(count):
        tk_ref[l] = dot(wk_ref[...], xs_ref[l * ROWS : (l + 1) * ROWS, :], NT)
    ones_lane = lax.broadcasted_iota(jnp.int32, (TOKENS, LANES), 1) == HEAD_DIM
    v_ref[...] = jnp.where(ones_lane, 1.0, 0.0).astype(BF16)

    def one_latent(l, carry):
        ft = ft_ref[l]
        f = jnp.transpose(ft.astype(F32)).astype(BF16)
        lane = lax.broadcasted_iota(jnp.int32, (TOKENS, LANES), 1)
        column = jnp.sum(jnp.where(lane == l, rcol_ref[...], 0.0), axis=1, keepdims=True)
        top = pl.multiple_of(l * ROWS, ROWS)
        tq = tq_ref[pl.ds(top, ROWS), :]
        tv = tv_ref[pl.ds(top, ROWS), :]
        tk = tk_ref[l]
        q_ref[...] = (dot(f, tq[:BASE].astype(BF16)) * column + tq[BASE : BASE + 1]).astype(BF16)
        v_ref[:, :HEAD_DIM] = (dot(f, tv[:BASE].astype(BF16)) * column + tv[BASE : BASE + 1]).astype(BF16)
        kt_ref[...] = (
            dot(tk[:, :BASE].astype(BF16), ft) * rstd_ref[pl.ds(l, 1), :] + tk[:, BASE : BASE + 1]
        ).astype(BF16)
        def one_block(j, carry):
            rows = pl.ds(pl.multiple_of(j * Q_ROWS, Q_ROWS), Q_ROWS)
            scores = dot(q_ref[rows, :], kt_ref[...])
            weights = jnp.exp2(scores - jnp.max(scores, axis=1, keepdims=True)).astype(BF16)
            mixed = dot(weights, v_ref[...])
            own_ref[l, rows, :] = (mixed / mixed[:, HEAD_DIM : HEAD_DIM + 1]).astype(BF16)
            return carry
        lax.fori_loop(0, TOKENS // Q_ROWS, one_block, 0)
        ring(me, lambda k, peer: send_out(l, k, peer).start())
        arrived[me, l] = own_ref[l, rows_of(me), :]
        return carry

    def rows_of(peer):
        return pl.ds(pl.multiple_of(peer * tokens, tokens), tokens)

    def send_out(l, k, peer):
        return remote(
            own_ref.at[l, rows_of(peer)], arrived.at[me, l], out_send.at[k, l], out_recv.at[me, l], {"seq": peer}
        )

    def wait_out(k, peer):
        def one(l, carry):
            remote(
                own_ref.at[l, rows_of(peer)], arrived.at[peer, l], out_send.at[k, l], out_recv.at[peer, l], {"seq": peer}
            ).wait()
            return carry

        lax.fori_loop(0, count, one, 0)

    lax.fori_loop(0, count, one_latent, 0)
    ring(me, wait_out)
    for l in range(count):
        heads = [arrived[h, l].astype(F32)[:, :HEAD_DIM] for h in range(HEADS)]
        out_ref[l * tokens : (l + 1) * tokens, :] = jnp.concatenate(heads, axis=1).astype(BF16)


def attend(lat, cols, patch, wq, wk, wv):
    count, channels, tokens = lat.shape
    pos = position_rows()
    centred = jnp.asarray((pos - pos.mean(axis=1, keepdims=True)).astype(np.float32))
    vmem = pl.BlockSpec(memory_space=pltpu.VMEM)
    return pl.pallas_call(
        attend_kernel,
        out_shape=(jax.ShapeDtypeStruct((count * tokens, D), BF16), jax.ShapeDtypeStruct((8, count, D), F32)),
        in_specs=[vmem] * 7,
        out_specs=(vmem, vmem),
        scratch_shapes=[
            pltpu.VMEM((HEADS, count, channels, tokens), BF16),
            pltpu.VMEM((HEADS,) + cols.shape, F32),
            pltpu.VMEM((HEADS, count, tokens, LANES), BF16),
            pltpu.VMEM((count, TOKENS, LANES), BF16),
        ]
        + [pltpu.SemaphoreType.DMA((HEADS,))] * 4
        + [pltpu.SemaphoreType.DMA((HEADS, count))] * 2
        + [
            pltpu.VMEM((count, BASE, TOKENS), BF16),
            pltpu.VMEM((BASE, D), F32),
            pltpu.VMEM((count * ROWS, D), BF16),
            pltpu.VMEM((count * ROWS, HEAD_DIM), F32),
            pltpu.VMEM((count * ROWS, HEAD_DIM), F32),
            pltpu.VMEM((count, HEAD_DIM, ROWS), F32),
            pltpu.VMEM((LANES, TOKENS), F32),
            pltpu.VMEM((TOKENS, LANES), F32),
            pltpu.VMEM((TOKENS, HEAD_DIM), BF16),
            pltpu.VMEM((TOKENS, LANES), BF16),
            pltpu.VMEM((HEAD_DIM, TOKENS), BF16),
        ],
        compiler_params=pltpu.CompilerParams(collective_id=1, has_side_effects=True),
        cost_estimate=pl.CostEstimate(flops=8 * 10**9, bytes_accessed=4 * 10**6, transcendentals=6 * 10**6),
    )(lat, cols, patch, centred, wq, wk, wv)


def feed_forward_kernel(
    guidance_ref, state_ref, mods_ref, stacked_ref, out_w_ref,
    out_ref, fc1_ref, fc2_ref, normed_ref, theirs_ref, part_ref, got_ref, total_ref, noise_ref, partner_ref,
    load_sem, send_sem, recv_sem,
):
    side = lax.axis_index("cfg")
    peer = {"cfg": 1 - side}
    count = mods_ref.shape[1]
    tokens = state_ref.shape[0] // count
    units = fc1_ref.shape[1]
    barrier = pltpu.get_barrier_semaphore()
    pl.semaphore_signal(barrier, inc=1, device_id=peer, device_id_type=MESH)
    loads = [
        pltpu.make_async_copy(stacked_ref.at[:, n * units : (n + 1) * units, :], target, load_sem.at[n])
        for n, target in enumerate((fc1_ref, fc2_ref))
    ]
    for load in loads:
        load.start()
    for l in range(count):
        rows = slice(l * tokens, (l + 1) * tokens)
        normed_ref[rows, :] = (
            layer_norm(state_ref[rows, :]) * (1.0 + mods_ref[4, l : l + 1, :]) + mods_ref[3, l : l + 1, :]
        ).astype(BF16)
    pl.semaphore_wait(barrier, 1)
    hand = remote(normed_ref, theirs_ref, send_sem.at[0], recv_sem.at[0], peer)
    hand.start()

    def half_of(source_ref, target_ref):
        target_ref[...] = jnp.zeros_like(target_ref)

        def one(g, carry):
            group = pl.ds(pl.multiple_of(g * 8, 8), 8)
            hidden = dot(source_ref[...], fc1_ref[group].reshape(8 * units, D), NT)
            hidden = jax.nn.gelu(hidden, approximate=True).astype(BF16)
            target_ref[...] += dot(hidden, fc2_ref[group].reshape(8 * units, D))
            return carry

        lax.fori_loop(0, HEADS // 8, one, 0)

    for load in loads:
        load.wait()
    hand.wait()
    half_of(theirs_ref, part_ref)
    back = remote(part_ref, got_ref, send_sem.at[1], recv_sem.at[1], peer)
    back.start()
    half_of(normed_ref, total_ref)
    back.wait()
    for l in range(count):
        rows = slice(l * tokens, (l + 1) * tokens)
        state = state_ref[rows, :] + mods_ref[5, l : l + 1, :] * (total_ref[rows, :] + got_ref[rows, :])
        normed_ref[rows, :] = (
            layer_norm(state) * (1.0 + mods_ref[7, l : l + 1, :]) + mods_ref[6, l : l + 1, :]
        ).astype(BF16)
    noise_ref[...] = dot(out_w_ref[...], normed_ref[...], (((0,), (1,)), ((), ())))
    last = remote(
        noise_ref.at[pl.ds(pl.multiple_of((1 - side) * 8, 8), 8)], partner_ref, send_sem.at[2], recv_sem.at[2], peer
    )
    last.start()
    last.wait()
    own = noise_ref[pl.ds(pl.multiple_of(side * 8, 8), 8), :]
    cond_noise = jnp.where(side == 0, own, partner_ref[...])
    free_noise = jnp.where(side == 0, partner_ref[...], own)
    out_ref[...] = free_noise + guidance_ref[0] * (cond_noise - free_noise)


def feed_forward(state, mods, stacked, w_out, guidance, units):
    tokens = state.shape[0]
    whole = pl.BlockSpec(memory_space=pltpu.VMEM)
    return pl.pallas_call(
        feed_forward_kernel,
        out_shape=jax.ShapeDtypeStruct((8, tokens), F32),
        in_specs=[pl.BlockSpec(memory_space=pltpu.SMEM), whole, whole, pl.BlockSpec(memory_space=pl.ANY), whole],
        out_specs=whole,
        scratch_shapes=[
            pltpu.VMEM((HEADS, units, D), BF16),
            pltpu.VMEM((HEADS, units, D), BF16),
            pltpu.VMEM((tokens, D), BF16),
            pltpu.VMEM((tokens, D), BF16),
            pltpu.VMEM((tokens, D), F32),
            pltpu.VMEM((tokens, D), F32),
            pltpu.VMEM((tokens, D), F32),
            pltpu.VMEM((16, tokens), F32),
            pltpu.VMEM((8, tokens), F32),
            pltpu.SemaphoreType.DMA((2,)),
            pltpu.SemaphoreType.DMA((3,)),
            pltpu.SemaphoreType.DMA((3,)),
        ],
        compiler_params=pltpu.CompilerParams(collective_id=0, has_side_effects=True),
        cost_estimate=pl.CostEstimate(flops=8 * 10**9, bytes_accessed=12 * 10**6, transcendentals=2 * 10**6),
    )(guidance, state, mods, stacked, w_out)


def shards(
    latents, timesteps, labels, guidance, keep_coef, noise_coef, w_patch, label_table,
    w_time1, w_time2, ada_weight, w_qkv, w_proj, w_fc1, w_fc2, w_out,
):
    count, tok_count, channels = latents.shape
    side = lax.axis_index("cfg")
    place = lax.axis_index("seq")
    half = w_fc2.shape[0] // 2
    fc1_half = lax.dynamic_slice_in_dim(w_fc1.T, side * half, half, 0)
    fc2_half = lax.dynamic_slice_in_dim(w_fc2, side * half, half, 0)
    stacked = lax.all_gather(jnp.concatenate([fc1_half, fc2_half, w_proj.T], axis=0), "seq", axis=0)
    proj_full = stacked[:, 2 * half :].reshape(D, D)

    classes = jnp.where(side == 0, labels, CLASSES)
    steps_all = lax.all_gather(timesteps, "lat", axis=0, tiled=True)
    waves = time_waves(steps_all).astype(BF16)
    hidden_own = jax.nn.silu(dot(waves, w_time1)).astype(BF16)
    hidden_time = lax.all_gather(hidden_own, "lat", axis=1, tiled=True)
    vector_own = dot(hidden_time, w_time2)
    vector = lax.all_to_all(vector_own, "lat", split_axis=0, concat_axis=1, tiled=True)
    onehot = (classes[:, None] == jnp.arange(CLASSES + 1, dtype=jnp.int32)[None, :]).astype(BF16)
    conditioning = vector + dot(onehot, label_table)
    own_columns = dot(jax.nn.silu(conditioning).astype(BF16), ada_weight)
    lat_t = jnp.transpose(latents, (0, 2, 1)).astype(BF16)
    blocks = w_qkv.T.reshape(3, HEAD_DIM, D)
    got = jnp.stack(
        [
            lax.ppermute(blocks[j], "seq", [(s, (3 * s + j) % HEADS) for s in range(HEADS)])
            for j in range(3)
        ]
    )
    head_w = [lax.dynamic_index_in_dim(got, (HEADS * kind + place) % 3, 0, False) for kind in range(3)]
    attended, mods = attend(lat_t, own_columns, w_patch, *head_w)

    pos = jnp.asarray(position_rows().astype(np.float32))
    columns = pos[:GRID]
    lines = lax.dynamic_slice_in_dim(pos, GRID + place * (tok_count // GRID), tok_count // GRID, 0)
    own_pos = (columns[None] + lines[:, None]).reshape(tok_count, D)
    state = dot(latents.reshape(-1, channels).astype(BF16), w_patch).reshape(count, tok_count, D) + own_pos[None]
    projected = dot(attended, proj_full, NT).reshape(count, tok_count, D)
    state = state + mods[2][:, None, :] * projected
    guided = feed_forward(state.reshape(-1, D), mods, stacked, w_out, guidance, half)
    half_width = channels // 2
    own_latent = lax.dynamic_slice_in_dim(latents, side * half_width, half_width, 2)
    guided = guided.T.reshape(count, tok_count, half_width)
    return keep_coef[:, None, None] * own_latent + noise_coef[:, None, None] * guided


def solution(mesh):
    return jax.shard_map(
        shards,
        mesh=mesh,
        in_specs=(
            P("lat", "seq", None), P("lat"), P("lat"), P(), P("lat"), P("lat"), P(), P(),
            P(None, "lat"), P(None, "lat"), P(None, "seq"), P(None, "seq"), P(None, "seq"),
            P(None, "seq"), P("seq", None), P(),
        ),
        out_specs=P("lat", "seq", "cfg"),
        check_vma=False,
    )
```

```python
import math

import jax
import jax.numpy as jnp
import numpy as np
from jax import lax
from jax.experimental import pallas as pl
from jax.experimental.pallas import tpu as pltpu
from jax.sharding import PartitionSpec as P

D = 1152
HEADS = 16
HEAD_DIM = 72
CLASSES = 1000
FREQ = 256
GRID = 32
TOKENS = 1024
BASE = 16 + 2 * GRID
ROWS = 96
LANES = 128
Q_ROWS = 256
F32 = jnp.float32
BF16 = jnp.bfloat16
NT = (((1,), (1,)), ((), ()))
NN = (((1,), (0,)), ((), ()))
MESH = pl.DeviceIdType.MESH
HIGH = lax.Precision.HIGHEST


def position_rows():
    quarter = D // 4
    frequency = np.exp(-math.log(10000.0) * np.arange(quarter) / quarter)
    angle = np.arange(GRID)[:, None] * frequency[None, :]
    waves = np.concatenate([np.sin(angle), np.cos(angle)], axis=1)
    rows = np.zeros((2 * GRID, D))
    rows[:GRID, : D // 2] = waves
    rows[GRID:, D // 2 :] = waves
    return rows


def dot(a, b, dims=NN, precision=None):
    return lax.dot_general(a, b, dims, precision=precision, preferred_element_type=F32)


def layer_norm(values):
    average = jnp.mean(values, axis=-1, keepdims=True)
    centered = values - average
    spread = jnp.mean(centered * centered, axis=-1, keepdims=True)
    return centered * lax.rsqrt(spread + 1e-06)


def time_waves(timesteps):
    half_count = FREQ // 2
    frequency = jnp.exp(-math.log(10000.0) * jnp.arange(half_count, dtype=F32) / half_count)
    angles = timesteps.astype(F32)[:, None] * frequency[None, :]
    return jnp.concatenate([jnp.cos(angles), jnp.sin(angles)], axis=-1)


def ring(me, body):
    def one(k, carry):
        body(k, lax.rem(me + k, HEADS))
        return carry

    lax.fori_loop(1, HEADS, one, 0)


def remote(source, target, send_sem, recv_sem, peer):
    return pltpu.make_async_remote_copy(
        src_ref=source, dst_ref=target, send_sem=send_sem, recv_sem=recv_sem, device_id=peer, device_id_type=MESH
    )


def attend_kernel(
    lat_ref, cols_ref, patch_ref, pos_ref, wq_ref, wk_ref, wv_ref,
    out_ref, mods_ref,
    lat_all, cols_all, arrived, own_ref, lat_send, lat_recv, cols_send, cols_recv, out_send, out_recv,
    ft_ref, base_ref, xs_ref, tq_ref, tv_ref, tk_ref, rstd_ref, rcol_ref, q_ref, v_ref, kt_ref,
):
    count = lat_ref.shape[0]
    tokens = lat_ref.shape[2]
    me = lax.axis_index("seq")
    barrier = pltpu.get_barrier_semaphore()
    ring(me, lambda k, peer: pl.semaphore_signal(barrier, inc=1, device_id={"seq": peer}, device_id_type=MESH))
    pl.semaphore_wait(barrier, HEADS - 1)

    def send_inputs(k, peer):
        remote(cols_ref, cols_all.at[me], cols_send.at[k], cols_recv.at[me], {"seq": peer}).start()
        remote(lat_ref, lat_all.at[me], lat_send.at[k], lat_recv.at[me], {"seq": peer}).start()

    def wait_inputs(k, peer):
        remote(cols_ref, cols_all.at[peer], cols_send.at[k], cols_recv.at[peer], {"seq": peer}).wait()
        remote(lat_ref, lat_all.at[peer], lat_send.at[k], lat_recv.at[peer], {"seq": peer}).wait()

    ring(me, send_inputs)
    lat_all[me] = lat_ref[...]
    cols_all[me] = cols_ref[...]
    patch = patch_ref[...].astype(F32)
    base_ref[:16, :] = patch - jnp.mean(patch, axis=1, keepdims=True)
    base_ref[16:, :] = pos_ref[...]
    base = base_ref[...]
    gram = dot(base, base, NT, HIGH) * (1.0 / D)
    token = lax.broadcasted_iota(jnp.int32, (2 * GRID, TOKENS), 1)
    place = lax.broadcasted_iota(jnp.int32, (2 * GRID, TOKENS), 0)
    hot = jnp.where(jnp.where(place < GRID, token % GRID, token // GRID + GRID) == place, 1.0, 0.0).astype(BF16)
    rstd_ref[...] = jnp.zeros_like(rstd_ref)
    ring(me, wait_inputs)
    for n in range(8):
        mods_ref[n] = jnp.concatenate([cols_all[2 * n], cols_all[2 * n + 1]], axis=1)
    for l in range(count):
        for n in range(HEADS // 2):
            pair = [lat_all[2 * n + m, l].astype(F32) for m in range(2)]
            ft_ref[l, :16, n * LANES : (n + 1) * LANES] = jnp.concatenate(pair, axis=1).astype(BF16)
        ft_ref[l, 16:, :] = hot
        ft = ft_ref[l].astype(F32)
        spread = jnp.sum(dot(gram, ft, NN, HIGH) * ft, axis=0, keepdims=True)
        rstd_ref[l : l + 1, :] = lax.rsqrt(spread + 1e-06)
        xs_ref[l * ROWS : l * ROWS + BASE, :] = (base * (1.0 + mods_ref[1, l : l + 1, :])).astype(BF16)
        xs_ref[l * ROWS + BASE : (l + 1) * ROWS, :] = jnp.broadcast_to(
            mods_ref[0, l : l + 1, :], (ROWS - BASE, D)
        ).astype(BF16)
    rcol_ref[...] = jnp.transpose(rstd_ref[...])
    factor = math.log2(math.e) / math.sqrt(HEAD_DIM)
    tq_ref[...] = dot(xs_ref[...], wq_ref[...], NT) * factor
    tv_ref[...] = dot(xs_ref[...], wv_ref[...], NT)
    for l in range(count):
        tk_ref[l] = dot(wk_ref[...], xs_ref[l * ROWS : (l + 1) * ROWS, :], NT)
    ones_lane = lax.broadcasted_iota(jnp.int32, (TOKENS, LANES), 1) == HEAD_DIM
    v_ref[...] = jnp.where(ones_lane, 1.0, 0.0).astype(BF16)

    def one_latent(p, m):
        l = 2 * p + m
        ft = ft_ref[l]
        f = jnp.transpose(ft.astype(F32)).astype(BF16)
        lane = lax.broadcasted_iota(jnp.int32, (TOKENS, LANES), 1)
        column = jnp.sum(jnp.where(lane == l, rcol_ref[...], 0.0), axis=1, keepdims=True)
        top = pl.multiple_of(l * ROWS, ROWS)
        tq = tq_ref[pl.ds(top, ROWS), :]
        tv = tv_ref[pl.ds(top, ROWS), :]
        tk = tk_ref[l]
        q_ref[...] = (dot(f, tq[:BASE].astype(BF16)) * column + tq[BASE : BASE + 1]).astype(BF16)
        v_ref[:, :HEAD_DIM] = (dot(f, tv[:BASE].astype(BF16)) * column + tv[BASE : BASE + 1]).astype(BF16)
        kt_ref[...] = (
            dot(tk[:, :BASE].astype(BF16), ft) * rstd_ref[pl.ds(l, 1), :] + tk[:, BASE : BASE + 1]
        ).astype(BF16)
        def one_block(j, carry):
            rows = pl.ds(pl.multiple_of(j * Q_ROWS, Q_ROWS), Q_ROWS)
            scores = dot(q_ref[rows, :], kt_ref[...])
            weights = jnp.exp2(scores - jnp.max(scores, axis=1, keepdims=True)).astype(BF16)
            mixed = dot(weights, v_ref[...])
            mixed = jnp.transpose(mixed / mixed[:, HEAD_DIM : HEAD_DIM + 1])[:HEAD_DIM]
            for t in range(Q_ROWS // tokens):
                own_ref[p, j * (Q_ROWS // tokens) + t, :, m * tokens : (m + 1) * tokens] = mixed[
                    :, t * tokens : (t + 1) * tokens
                ].astype(BF16)
            return carry
        lax.fori_loop(0, TOKENS // Q_ROWS, one_block, 0)

    def one_pair(p, carry):
        one_latent(p, 0)
        one_latent(p, 1)
        ring(me, lambda k, peer: send_out(p, k, peer).start())
        arrived[me, p] = own_ref[p, me]
        return carry

    def send_out(p, k, peer):
        return remote(own_ref.at[p, peer], arrived.at[me, p], out_send.at[k, p], out_recv.at[me, p], {"seq": peer})

    def wait_out(k, peer):
        for p in range(count // 2):
            remote(
                own_ref.at[p, peer], arrived.at[peer, p], out_send.at[k, p], out_recv.at[peer, p], {"seq": peer}
            ).wait()

    lax.fori_loop(0, count // 2, one_pair, 0)
    ring(me, wait_out)
    for p in range(count // 2):
        heads = jnp.concatenate([arrived[h, p].astype(F32) for h in range(HEADS)], axis=0)
        out_ref[2 * p * tokens : 2 * (p + 1) * tokens, :] = jnp.transpose(heads).astype(BF16)


def attend(lat, cols, patch, wq, wk, wv):
    count, channels, tokens = lat.shape
    pos = position_rows()
    centred = jnp.asarray((pos - pos.mean(axis=1, keepdims=True)).astype(np.float32))
    vmem = pl.BlockSpec(memory_space=pltpu.VMEM)
    return pl.pallas_call(
        attend_kernel,
        out_shape=(jax.ShapeDtypeStruct((count * tokens, D), BF16), jax.ShapeDtypeStruct((8, count, D), F32)),
        in_specs=[vmem] * 7,
        out_specs=(vmem, vmem),
        scratch_shapes=[
            pltpu.VMEM((HEADS, count, channels, tokens), BF16),
            pltpu.VMEM((HEADS,) + cols.shape, F32),
            pltpu.VMEM((HEADS, count // 2, HEAD_DIM, 2 * tokens), BF16),
            pltpu.VMEM((count // 2, HEADS, HEAD_DIM, 2 * tokens), BF16),
        ]
        + [pltpu.SemaphoreType.DMA((HEADS,))] * 4
        + [pltpu.SemaphoreType.DMA((HEADS, count // 2))] * 2
        + [
            pltpu.VMEM((count, BASE, TOKENS), BF16),
            pltpu.VMEM((BASE, D), F32),
            pltpu.VMEM((count * ROWS, D), BF16),
            pltpu.VMEM((count * ROWS, HEAD_DIM), F32),
            pltpu.VMEM((count * ROWS, HEAD_DIM), F32),
            pltpu.VMEM((count, HEAD_DIM, ROWS), F32),
            pltpu.VMEM((LANES, TOKENS), F32),
            pltpu.VMEM((TOKENS, LANES), F32),
            pltpu.VMEM((TOKENS, HEAD_DIM), BF16),
            pltpu.VMEM((TOKENS, LANES), BF16),
            pltpu.VMEM((HEAD_DIM, TOKENS), BF16),
        ],
        compiler_params=pltpu.CompilerParams(collective_id=1, has_side_effects=True),
        cost_estimate=pl.CostEstimate(flops=8 * 10**9, bytes_accessed=4 * 10**6, transcendentals=6 * 10**6),
    )(lat, cols, patch, centred, wq, wk, wv)


def feed_forward_kernel(
    guidance_ref, attended_ref, start_ref, mods_ref, stacked_ref, out_w_ref,
    out_ref, proj_ref, fc1_ref, fc2_ref, state_ref, normed_ref, theirs_ref, part_ref, got_ref, total_ref, noise_ref, partner_ref,
    load_sem, send_sem, recv_sem,
):
    side = lax.axis_index("cfg")
    peer = {"cfg": 1 - side}
    count = mods_ref.shape[1]
    tokens = start_ref.shape[0] // count
    units = fc1_ref.shape[1]
    barrier = pltpu.get_barrier_semaphore()
    pl.semaphore_signal(barrier, inc=1, device_id=peer, device_id_type=MESH)
    loads = [
        pltpu.make_async_copy(stacked_ref.at[:, first : first + target.shape[1], :], target, load_sem.at[n])
        for n, (first, target) in enumerate(((2 * units, proj_ref), (0, fc1_ref), (units, fc2_ref)))
    ]
    for load in loads:
        load.start()
    loads[0].wait()
    total_ref[...] = dot(attended_ref[...], proj_ref[...].reshape(D, D), NT)
    for l in range(count):
        rows = slice(l * tokens, (l + 1) * tokens)
        state_ref[rows, :] = start_ref[rows, :] + mods_ref[2, l : l + 1, :] * total_ref[rows, :]
        normed_ref[rows, :] = (
            layer_norm(state_ref[rows, :]) * (1.0 + mods_ref[4, l : l + 1, :]) + mods_ref[3, l : l + 1, :]
        ).astype(BF16)
    pl.semaphore_wait(barrier, 1)
    hand = remote(normed_ref, theirs_ref, send_sem.at[0], recv_sem.at[0], peer)
    hand.start()

    def half_of(source_ref, target_ref):
        target_ref[...] = jnp.zeros_like(target_ref)

        def one(g, carry):
            group = pl.ds(pl.multiple_of(g * 8, 8), 8)
            hidden = dot(source_ref[...], fc1_ref[group].reshape(8 * units, D), NT)
            hidden = jax.nn.gelu(hidden, approximate=True).astype(BF16)
            target_ref[...] += dot(hidden, fc2_ref[group].reshape(8 * units, D))
            return carry

        lax.fori_loop(0, HEADS // 8, one, 0)

    for load in loads[1:]:
        load.wait()
    hand.wait()
    half_of(theirs_ref, part_ref)
    back = remote(part_ref, got_ref, send_sem.at[1], recv_sem.at[1], peer)
    back.start()
    half_of(normed_ref, total_ref)
    back.wait()
    for l in range(count):
        rows = slice(l * tokens, (l + 1) * tokens)
        state = state_ref[rows, :] + mods_ref[5, l : l + 1, :] * (total_ref[rows, :] + got_ref[rows, :])
        normed_ref[rows, :] = (
            layer_norm(state) * (1.0 + mods_ref[7, l : l + 1, :]) + mods_ref[6, l : l + 1, :]
        ).astype(BF16)
    noise_ref[...] = dot(out_w_ref[...], normed_ref[...], (((0,), (1,)), ((), ())))
    last = remote(
        noise_ref.at[pl.ds(pl.multiple_of((1 - side) * 8, 8), 8)], partner_ref, send_sem.at[2], recv_sem.at[2], peer
    )
    last.start()
    last.wait()
    own = noise_ref[pl.ds(pl.multiple_of(side * 8, 8), 8), :]
    cond_noise = jnp.where(side == 0, own, partner_ref[...])
    free_noise = jnp.where(side == 0, partner_ref[...], own)
    out_ref[...] = free_noise + guidance_ref[0] * (cond_noise - free_noise)


def feed_forward(attended, state, mods, stacked, w_out, guidance, units):
    tokens = state.shape[0]
    whole = pl.BlockSpec(memory_space=pltpu.VMEM)
    return pl.pallas_call(
        feed_forward_kernel,
        out_shape=jax.ShapeDtypeStruct((8, tokens), F32),
        in_specs=[pl.BlockSpec(memory_space=pltpu.SMEM), whole, whole, whole, pl.BlockSpec(memory_space=pl.ANY), whole],
        out_specs=whole,
        scratch_shapes=[
            pltpu.VMEM((HEADS, HEAD_DIM, D), BF16),
            pltpu.VMEM((HEADS, units, D), BF16),
            pltpu.VMEM((HEADS, units, D), BF16),
            pltpu.VMEM((tokens, D), F32),
            pltpu.VMEM((tokens, D), BF16),
            pltpu.VMEM((tokens, D), BF16),
            pltpu.VMEM((tokens, D), F32),
            pltpu.VMEM((tokens, D), F32),
            pltpu.VMEM((tokens, D), F32),
            pltpu.VMEM((16, tokens), F32),
            pltpu.VMEM((8, tokens), F32),
            pltpu.SemaphoreType.DMA((3,)),
            pltpu.SemaphoreType.DMA((3,)),
            pltpu.SemaphoreType.DMA((3,)),
        ],
        compiler_params=pltpu.CompilerParams(collective_id=0, has_side_effects=True),
        cost_estimate=pl.CostEstimate(flops=8 * 10**9, bytes_accessed=12 * 10**6, transcendentals=2 * 10**6),
    )(guidance, attended, state, mods, stacked, w_out)


def shards(
    latents, timesteps, labels, guidance, keep_coef, noise_coef, w_patch, label_table,
    w_time1, w_time2, ada_weight, w_qkv, w_proj, w_fc1, w_fc2, w_out,
):
    count, tok_count, channels = latents.shape
    side = lax.axis_index("cfg")
    place = lax.axis_index("seq")
    half = w_fc2.shape[0] // 2
    fc1_half = lax.dynamic_slice_in_dim(w_fc1.T, side * half, half, 0)
    fc2_half = lax.dynamic_slice_in_dim(w_fc2, side * half, half, 0)
    stacked = lax.all_gather(jnp.concatenate([fc1_half, fc2_half, w_proj.T], axis=0), "seq", axis=0)

    classes = jnp.where(side == 0, labels, CLASSES)
    steps_all = lax.all_gather(timesteps, "lat", axis=0, tiled=True)
    waves = time_waves(steps_all).astype(BF16)
    hidden_own = jax.nn.silu(dot(waves, w_time1)).astype(BF16)
    hidden_time = lax.all_gather(hidden_own, "lat", axis=1, tiled=True)
    vector_own = dot(hidden_time, w_time2)
    vector = lax.all_to_all(vector_own, "lat", split_axis=0, concat_axis=1, tiled=True)
    onehot = (classes[:, None] == jnp.arange(CLASSES + 1, dtype=jnp.int32)[None, :]).astype(BF16)
    conditioning = vector + dot(onehot, label_table)
    own_columns = dot(jax.nn.silu(conditioning).astype(BF16), ada_weight)
    lat_t = jnp.transpose(latents, (0, 2, 1)).astype(BF16)
    blocks = w_qkv.T.reshape(3, HEAD_DIM, D)
    got = jnp.stack(
        [
            lax.ppermute(blocks[j], "seq", [(s, (3 * s + j) % HEADS) for s in range(HEADS)])
            for j in range(3)
        ]
    )
    head_w = [lax.dynamic_index_in_dim(got, (HEADS * kind + place) % 3, 0, False) for kind in range(3)]
    attended, mods = attend(lat_t, own_columns, w_patch, *head_w)

    pos = jnp.asarray(position_rows().astype(np.float32))
    columns = pos[:GRID]
    lines = lax.dynamic_slice_in_dim(pos, GRID + place * (tok_count // GRID), tok_count // GRID, 0)
    own_pos = (columns[None] + lines[:, None]).reshape(tok_count, D)
    state = dot(latents.reshape(-1, channels).astype(BF16), w_patch).reshape(count, tok_count, D) + own_pos[None]
    guided = feed_forward(attended, state.reshape(-1, D), mods, stacked, w_out, guidance, half)
    half_width = channels // 2
    own_latent = lax.dynamic_slice_in_dim(latents, side * half_width, half_width, 2)
    guided = guided.T.reshape(count, tok_count, half_width)
    return keep_coef[:, None, None] * own_latent + noise_coef[:, None, None] * guided


def solution(mesh):
    return jax.shard_map(
        shards,
        mesh=mesh,
        in_specs=(
            P("lat", "seq", None), P("lat"), P("lat"), P(), P("lat"), P("lat"), P(), P(),
            P(None, "lat"), P(None, "lat"), P(None, "seq"), P(None, "seq"), P(None, "seq"),
            P(None, "seq"), P("seq", None), P(),
        ),
        out_specs=P("lat", "seq", "cfg"),
        check_vma=False,
    )
```

```python
import math

import jax
import jax.numpy as jnp
import numpy as np
from jax import lax
from jax.experimental import pallas as pl
from jax.experimental.pallas import tpu as pltpu
from jax.sharding import PartitionSpec as P

D = 1152
HEADS = 16
HEAD_DIM = 72
CLASSES = 1000
FREQ = 256
GRID = 32
TOKENS = 1024
BASE = 16 + 2 * GRID
ROWS = 96
LANES = 128
Q_ROWS = 256
F32 = jnp.float32
BF16 = jnp.bfloat16
NT = (((1,), (1,)), ((), ()))
NN = (((1,), (0,)), ((), ()))
MESH = pl.DeviceIdType.MESH
HIGH = lax.Precision.HIGHEST


def position_rows():
    quarter = D // 4
    frequency = np.exp(-math.log(10000.0) * np.arange(quarter) / quarter)
    angle = np.arange(GRID)[:, None] * frequency[None, :]
    waves = np.concatenate([np.sin(angle), np.cos(angle)], axis=1)
    rows = np.zeros((2 * GRID, D))
    rows[:GRID, : D // 2] = waves
    rows[GRID:, D // 2 :] = waves
    return rows


def dot(a, b, dims=NN, precision=None):
    return lax.dot_general(a, b, dims, precision=precision, preferred_element_type=F32)


def layer_norm(values):
    average = jnp.mean(values, axis=-1, keepdims=True)
    centered = values - average
    spread = jnp.mean(centered * centered, axis=-1, keepdims=True)
    return centered * lax.rsqrt(spread + 1e-06)


def time_waves(timesteps):
    half_count = FREQ // 2
    frequency = jnp.exp(-math.log(10000.0) * jnp.arange(half_count, dtype=F32) / half_count)
    angles = timesteps.astype(F32)[:, None] * frequency[None, :]
    return jnp.concatenate([jnp.cos(angles), jnp.sin(angles)], axis=-1)


def ring(me, body):
    def one(k, carry):
        body(k, lax.rem(me + k, HEADS))
        return carry

    lax.fori_loop(1, HEADS, one, 0)


def remote(source, target, send_sem, recv_sem, peer):
    return pltpu.make_async_remote_copy(
        src_ref=source, dst_ref=target, send_sem=send_sem, recv_sem=recv_sem, device_id=peer, device_id_type=MESH
    )


def attend_kernel(
    lat_ref, cols_ref, patch_ref, pos_ref, wq_ref, wk_ref, wv_ref,
    out_ref, mods_ref,
    lat_all, cols_all, arrived, own_ref, lat_send, lat_recv, cols_send, cols_recv, out_send, out_recv,
    ft_ref, base_ref, xs_ref, tq_ref, tv_ref, tk_ref, rstd_ref, rcol_ref, q_ref, v_ref, kt_ref,
):
    count = cols_ref.shape[0]
    tokens = lat_ref.shape[2] // 2
    me = lax.axis_index("seq")
    barrier = pltpu.get_barrier_semaphore()
    ring(me, lambda k, peer: pl.semaphore_signal(barrier, inc=1, device_id={"seq": peer}, device_id_type=MESH))
    pl.semaphore_wait(barrier, HEADS - 1)

    def send_inputs(k, peer):
        remote(cols_ref, cols_all.at[me], cols_send.at[k], cols_recv.at[me], {"seq": peer}).start()
        remote(lat_ref, lat_all.at[me], lat_send.at[k], lat_recv.at[me], {"seq": peer}).start()

    def wait_inputs(k, peer):
        remote(cols_ref, cols_all.at[peer], cols_send.at[k], cols_recv.at[peer], {"seq": peer}).wait()
        remote(lat_ref, lat_all.at[peer], lat_send.at[k], lat_recv.at[peer], {"seq": peer}).wait()

    ring(me, send_inputs)
    lat_all[me] = lat_ref[...]
    cols_all[me] = cols_ref[...]
    patch = patch_ref[...].astype(F32)
    base_ref[:16, :] = patch - jnp.mean(patch, axis=1, keepdims=True)
    base_ref[16:, :] = pos_ref[...]
    base = base_ref[...]
    gram = dot(base, base, NT, HIGH) * (1.0 / D)
    token = lax.broadcasted_iota(jnp.int32, (2 * GRID, TOKENS), 1)
    place = lax.broadcasted_iota(jnp.int32, (2 * GRID, TOKENS), 0)
    hot = jnp.where(jnp.where(place < GRID, token % GRID, token // GRID + GRID) == place, 1.0, 0.0).astype(BF16)
    rstd_ref[...] = jnp.zeros_like(rstd_ref)
    ring(me, wait_inputs)
    for n in range(8):
        mods_ref[n] = jnp.concatenate([cols_all[2 * n], cols_all[2 * n + 1]], axis=1)
    for l in range(count):
        for n in range(HEADS // 2):
            side = slice(l % 2 * tokens, (l % 2 + 1) * tokens)
            pair = [lat_all[2 * n + m, l // 2].astype(F32)[:, side] for m in range(2)]
            ft_ref[l, :16, n * LANES : (n + 1) * LANES] = jnp.concatenate(pair, axis=1).astype(BF16)
        ft_ref[l, 16:, :] = hot
        ft = ft_ref[l].astype(F32)
        spread = jnp.sum(dot(gram, ft, NN, HIGH) * ft, axis=0, keepdims=True)
        rstd_ref[l : l + 1, :] = lax.rsqrt(spread + 1e-06)
        xs_ref[l * ROWS : l * ROWS + BASE, :] = (base * (1.0 + mods_ref[1, l : l + 1, :])).astype(BF16)
        xs_ref[l * ROWS + BASE : (l + 1) * ROWS, :] = jnp.broadcast_to(
            mods_ref[0, l : l + 1, :], (ROWS - BASE, D)
        ).astype(BF16)
    rcol_ref[...] = jnp.transpose(rstd_ref[...])
    factor = math.log2(math.e) / math.sqrt(HEAD_DIM)
    tq_ref[...] = dot(xs_ref[...], wq_ref[...], NT) * factor
    tv_ref[...] = dot(xs_ref[...], wv_ref[...], NT)
    for l in range(count):
        tk_ref[l] = dot(wk_ref[...], xs_ref[l * ROWS : (l + 1) * ROWS, :], NT)
    ones_lane = lax.broadcasted_iota(jnp.int32, (TOKENS, LANES), 1) == HEAD_DIM
    v_ref[...] = jnp.where(ones_lane, 1.0, 0.0).astype(BF16)

    def one_latent(p, m):
        l = 2 * p + m
        ft = ft_ref[l]
        f = jnp.transpose(ft.astype(F32)).astype(BF16)
        lane = lax.broadcasted_iota(jnp.int32, (TOKENS, LANES), 1)
        column = jnp.sum(jnp.where(lane == l, rcol_ref[...], 0.0), axis=1, keepdims=True)
        top = pl.multiple_of(l * ROWS, ROWS)
        tq = tq_ref[pl.ds(top, ROWS), :]
        tv = tv_ref[pl.ds(top, ROWS), :]
        tk = tk_ref[l]
        q_ref[...] = (dot(f, tq[:BASE].astype(BF16)) * column + tq[BASE : BASE + 1]).astype(BF16)
        v_ref[:, :HEAD_DIM] = (dot(f, tv[:BASE].astype(BF16)) * column + tv[BASE : BASE + 1]).astype(BF16)
        kt_ref[...] = (
            dot(tk[:, :BASE].astype(BF16), ft) * rstd_ref[pl.ds(l, 1), :] + tk[:, BASE : BASE + 1]
        ).astype(BF16)
        def one_block(j, carry):
            rows = pl.ds(pl.multiple_of(j * Q_ROWS, Q_ROWS), Q_ROWS)
            scores = dot(q_ref[rows, :], kt_ref[...])
            weights = jnp.exp2(scores - jnp.max(scores, axis=1, keepdims=True)).astype(BF16)
            mixed = dot(weights, v_ref[...])
            mixed = jnp.transpose(mixed / mixed[:, HEAD_DIM : HEAD_DIM + 1])[:HEAD_DIM]
            for t in range(Q_ROWS // tokens):
                own_ref[p, j * (Q_ROWS // tokens) + t, :, m * tokens : (m + 1) * tokens] = mixed[
                    :, t * tokens : (t + 1) * tokens
                ].astype(BF16)
            return carry
        lax.fori_loop(0, TOKENS // Q_ROWS, one_block, 0)

    def one_pair(p, carry):
        one_latent(p, 0)
        one_latent(p, 1)
        ring(me, lambda k, peer: send_out(p, k, peer).start())
        arrived[me, p] = own_ref[p, me]
        return carry

    def send_out(p, k, peer):
        return remote(own_ref.at[p, peer], arrived.at[me, p], out_send.at[k, p], out_recv.at[me, p], {"seq": peer})

    def wait_out(k, peer):
        for p in range(count // 2):
            remote(
                own_ref.at[p, peer], arrived.at[peer, p], out_send.at[k, p], out_recv.at[peer, p], {"seq": peer}
            ).wait()

    lax.fori_loop(0, count // 2, one_pair, 0)
    ring(me, wait_out)
    for p in range(count // 2):
        heads = jnp.concatenate([arrived[h, p].astype(F32) for h in range(HEADS)], axis=0)
        out_ref[2 * p * tokens : 2 * (p + 1) * tokens, :] = jnp.transpose(heads).astype(BF16)


def attend(lat, cols, patch, wq, wk, wv):
    count = cols.shape[0]
    tokens = lat.shape[2] // 2
    pos = position_rows()
    centred = jnp.asarray((pos - pos.mean(axis=1, keepdims=True)).astype(np.float32))
    vmem = pl.BlockSpec(memory_space=pltpu.VMEM)
    return pl.pallas_call(
        attend_kernel,
        out_shape=(jax.ShapeDtypeStruct((count * tokens, D), BF16), jax.ShapeDtypeStruct((8, count, D), F32)),
        in_specs=[vmem] * 7,
        out_specs=(vmem, vmem),
        scratch_shapes=[
            pltpu.VMEM((HEADS,) + lat.shape, BF16),
            pltpu.VMEM((HEADS,) + cols.shape, F32),
            pltpu.VMEM((HEADS, count // 2, HEAD_DIM, 2 * tokens), BF16),
            pltpu.VMEM((count // 2, HEADS, HEAD_DIM, 2 * tokens), BF16),
        ]
        + [pltpu.SemaphoreType.DMA((HEADS,))] * 4
        + [pltpu.SemaphoreType.DMA((HEADS, count // 2))] * 2
        + [
            pltpu.VMEM((count, BASE, TOKENS), BF16),
            pltpu.VMEM((BASE, D), F32),
            pltpu.VMEM((count * ROWS, D), BF16),
            pltpu.VMEM((count * ROWS, HEAD_DIM), F32),
            pltpu.VMEM((count * ROWS, HEAD_DIM), F32),
            pltpu.VMEM((count, HEAD_DIM, ROWS), F32),
            pltpu.VMEM((LANES, TOKENS), F32),
            pltpu.VMEM((TOKENS, LANES), F32),
            pltpu.VMEM((TOKENS, HEAD_DIM), BF16),
            pltpu.VMEM((TOKENS, LANES), BF16),
            pltpu.VMEM((HEAD_DIM, TOKENS), BF16),
        ],
        compiler_params=pltpu.CompilerParams(collective_id=1, has_side_effects=True),
        cost_estimate=pl.CostEstimate(flops=8 * 10**9, bytes_accessed=4 * 10**6, transcendentals=6 * 10**6),
    )(lat, cols, patch, centred, wq, wk, wv)


def feed_forward_kernel(
    guidance_ref, attended_ref, start_ref, mods_ref, stacked_ref, out_w_ref,
    out_ref, proj_ref, fc1_ref, fc2_ref, state_ref, normed_ref, theirs_ref, part_ref, got_ref, total_ref, noise_ref, partner_ref,
    load_sem, send_sem, recv_sem,
):
    side = lax.axis_index("cfg")
    peer = {"cfg": 1 - side}
    count = mods_ref.shape[1]
    tokens = start_ref.shape[0] // count
    units = fc1_ref.shape[1]
    barrier = pltpu.get_barrier_semaphore()
    pl.semaphore_signal(barrier, inc=1, device_id=peer, device_id_type=MESH)
    loads = [
        pltpu.make_async_copy(stacked_ref.at[:, first : first + target.shape[1], :], target, load_sem.at[n])
        for n, (first, target) in enumerate(((2 * units, proj_ref), (0, fc1_ref), (units, fc2_ref)))
    ]
    for load in loads:
        load.start()
    loads[0].wait()
    total_ref[...] = dot(attended_ref[...], proj_ref[...].reshape(D, D), NT)
    for l in range(count):
        rows = slice(l * tokens, (l + 1) * tokens)
        state_ref[rows, :] = start_ref[rows, :] + mods_ref[2, l : l + 1, :] * total_ref[rows, :]
        normed_ref[rows, :] = (
            layer_norm(state_ref[rows, :]) * (1.0 + mods_ref[4, l : l + 1, :]) + mods_ref[3, l : l + 1, :]
        ).astype(BF16)
    pl.semaphore_wait(barrier, 1)
    hand = remote(normed_ref, theirs_ref, send_sem.at[0], recv_sem.at[0], peer)
    hand.start()

    def half_of(source_ref, target_ref):
        target_ref[...] = jnp.zeros_like(target_ref)

        def one(g, carry):
            group = pl.ds(pl.multiple_of(g * 8, 8), 8)
            hidden = dot(source_ref[...], fc1_ref[group].reshape(8 * units, D), NT)
            hidden = jax.nn.gelu(hidden, approximate=True).astype(BF16)
            target_ref[...] += dot(hidden, fc2_ref[group].reshape(8 * units, D))
            return carry

        lax.fori_loop(0, HEADS // 8, one, 0)

    for load in loads[1:]:
        load.wait()
    hand.wait()
    half_of(theirs_ref, part_ref)
    back = remote(part_ref, got_ref, send_sem.at[1], recv_sem.at[1], peer)
    back.start()
    half_of(normed_ref, total_ref)
    back.wait()
    for l in range(count):
        rows = slice(l * tokens, (l + 1) * tokens)
        state = state_ref[rows, :] + mods_ref[5, l : l + 1, :] * (total_ref[rows, :] + got_ref[rows, :])
        normed_ref[rows, :] = (
            layer_norm(state) * (1.0 + mods_ref[7, l : l + 1, :]) + mods_ref[6, l : l + 1, :]
        ).astype(BF16)
    noise_ref[...] = dot(out_w_ref[...], normed_ref[...], (((0,), (1,)), ((), ())))
    last = remote(
        noise_ref.at[pl.ds(pl.multiple_of((1 - side) * 8, 8), 8)], partner_ref, send_sem.at[2], recv_sem.at[2], peer
    )
    last.start()
    last.wait()
    own = noise_ref[pl.ds(pl.multiple_of(side * 8, 8), 8), :]
    cond_noise = jnp.where(side == 0, own, partner_ref[...])
    free_noise = jnp.where(side == 0, partner_ref[...], own)
    out_ref[...] = free_noise + guidance_ref[0] * (cond_noise - free_noise)


def feed_forward(attended, state, mods, stacked, w_out, guidance, units):
    tokens = state.shape[0]
    whole = pl.BlockSpec(memory_space=pltpu.VMEM)
    return pl.pallas_call(
        feed_forward_kernel,
        out_shape=jax.ShapeDtypeStruct((8, tokens), F32),
        in_specs=[pl.BlockSpec(memory_space=pltpu.SMEM), whole, whole, whole, pl.BlockSpec(memory_space=pl.ANY), whole],
        out_specs=whole,
        scratch_shapes=[
            pltpu.VMEM((HEADS, HEAD_DIM, D), BF16),
            pltpu.VMEM((HEADS, units, D), BF16),
            pltpu.VMEM((HEADS, units, D), BF16),
            pltpu.VMEM((tokens, D), F32),
            pltpu.VMEM((tokens, D), BF16),
            pltpu.VMEM((tokens, D), BF16),
            pltpu.VMEM((tokens, D), F32),
            pltpu.VMEM((tokens, D), F32),
            pltpu.VMEM((tokens, D), F32),
            pltpu.VMEM((16, tokens), F32),
            pltpu.VMEM((8, tokens), F32),
            pltpu.SemaphoreType.DMA((3,)),
            pltpu.SemaphoreType.DMA((3,)),
            pltpu.SemaphoreType.DMA((3,)),
        ],
        compiler_params=pltpu.CompilerParams(collective_id=0, has_side_effects=True),
        cost_estimate=pl.CostEstimate(flops=8 * 10**9, bytes_accessed=12 * 10**6, transcendentals=2 * 10**6),
    )(guidance, attended, state, mods, stacked, w_out)


def shards(
    latents, timesteps, labels, guidance, keep_coef, noise_coef, w_patch, label_table,
    w_time1, w_time2, ada_weight, w_qkv, w_proj, w_fc1, w_fc2, w_out,
):
    count, tok_count, channels = latents.shape
    side = lax.axis_index("cfg")
    place = lax.axis_index("seq")
    half = w_fc2.shape[0] // 2
    parts = [jnp.concatenate([w_fc1.T[n : n + half], w_fc2[n : n + half], w_proj.T], axis=0) for n in (0, half)]
    stacked = lax.all_gather(jnp.where(side == 0, parts[0], parts[1]), "seq", axis=0)

    classes = jnp.where(side == 0, labels, CLASSES)
    steps_all = lax.all_gather(timesteps, "lat", axis=0, tiled=True)
    waves = time_waves(steps_all).astype(BF16)
    hidden_own = jax.nn.silu(dot(waves, w_time1)).astype(BF16)
    hidden_time = lax.all_gather(hidden_own, "lat", axis=1, tiled=True)
    vector_own = dot(hidden_time, w_time2)
    vector = lax.all_to_all(vector_own, "lat", split_axis=0, concat_axis=1, tiled=True)
    onehot = (classes[:, None] == jnp.arange(CLASSES + 1, dtype=jnp.int32)[None, :]).astype(BF16)
    conditioning = vector + dot(onehot, label_table)
    own_columns = dot(jax.nn.silu(conditioning).astype(BF16), ada_weight)
    lat_t = jnp.transpose(latents, (0, 2, 1)).astype(BF16)
    blocks = w_qkv.T.reshape(3, HEAD_DIM, D)
    got = jnp.stack(
        [
            lax.ppermute(blocks[j], "seq", [(s, (3 * s + j) % HEADS) for s in range(HEADS)])
            for j in range(3)
        ]
    )
    head_w = [lax.dynamic_index_in_dim(got, (HEADS * kind + place) % 3, 0, False) for kind in range(3)]
    attended, mods = attend(jnp.concatenate([lat_t[0::2], lat_t[1::2]], axis=2), own_columns, w_patch, *head_w)

    pos = jnp.asarray(position_rows().astype(np.float32))
    columns = pos[:GRID]
    lines = lax.dynamic_slice_in_dim(pos, GRID + place * (tok_count // GRID), tok_count // GRID, 0)
    own_pos = (columns[None] + lines[:, None]).reshape(tok_count, D)
    state = dot(latents.reshape(-1, channels).astype(BF16), w_patch).reshape(count, tok_count, D) + own_pos[None]
    guided = feed_forward(attended, state.reshape(-1, D), mods, stacked, w_out, guidance, half)
    half_width = channels // 2
    own_latent = lax.dynamic_slice_in_dim(latents, side * half_width, half_width, 2)
    guided = guided.T.reshape(count, tok_count, half_width)
    return keep_coef[:, None, None] * own_latent + noise_coef[:, None, None] * guided


def solution(mesh):
    return jax.shard_map(
        shards,
        mesh=mesh,
        in_specs=(
            P("lat", "seq", None), P("lat"), P("lat"), P(), P("lat"), P("lat"), P(), P(),
            P(None, "lat"), P(None, "lat"), P(None, "seq"), P(None, "seq"), P(None, "seq"),
            P(None, "seq"), P("seq", None), P(),
        ),
        out_specs=P("lat", "seq", "cfg"),
        check_vma=False,
    )
```
